32 devices in a mesh: group: 2 (over y), frame: 4 (over z), row: 2 (over x), head: 2 (over core).
Axes of the slice: x: 2, y: 2, z: 4, core: 2. Of those that a mesh axis runs over, the one named last changes fastest.
Arguments:
- q_video: bfloat16 [16, 16, 16, 1536], P(('group', 'frame'), 'row', None, 'head'), parts along dimension 0, may hold values from -16 to 16
- k_video: bfloat16 [16, 16, 16, 1536], P(('group', 'frame'), 'row', None, 'head'), parts along dimension 0, may hold values from -8 to 8
- v_video: bfloat16 [16, 16, 16, 1536], P(('group', 'frame'), 'row', None, 'head'), parts along dimension 0, may hold values from -6 to 6
- q_reg: bfloat16 [256, 1536], P('group', 'head'), parts along dimension 0, may hold values from -16 to 16
- k_reg: bfloat16 [256, 1536], P('group', 'head'), parts along dimension 0, may hold values from -6 to 6
- v_reg: bfloat16 [256, 1536], P('group', 'head'), parts along dimension 0, may hold values from -6 to 6
- nbr_mask: int32 [4, 2, 2, 26], P('frame', 'row'), may hold values 0 or 1
Outputs:
- out_video: bfloat16 [16, 16, 16, 1536], P(('group', 'frame'), 'row', None, 'head'), parts along dimension 0
- out_reg: bfloat16 [256, 1536], P(('group', 'frame', 'row'), 'head'), parts along dimension 0
The draws below stay inside these ranges and needn't reach their ends.
There are 2 independent parts, one for each index of `group`. The reference program is written for one: setup_inputs(seed, part) draws one part's arguments, and reference() takes and returns one part's arrays. A program takes and returns all parts, laid end to end along the dimension named above; an argument that names none is the same for every part. Nothing has to cross between parts.
All inputs are finite; a program needn't handle non-finite values. No bound on the sum of `nbr_mask` on one device may be relied on, other than what follows from the above.
Results may differ from the reference program's by a relative error of at most 0.0049.
Values may be sent and summed in bfloat16 or wider, within the bound.
A program may use at most 64 MiB of HBM per device.

```python
import jax
import jax.numpy as jnp
from jax import lax

HEADS = 12
HEAD_DIM = 128
TILE_F = 2
TILE_R = 8
TILE_C = 8
COL_TILES = 2
REGS = 128
NBRS = 26
FRAMES = 8
ROWS = 16
COLS = 16
N_FRAME = 4
N_ROW = 2


def draw_q_video(key, part):
    shape = (FRAMES, ROWS, COLS, HEADS * HEAD_DIM)
    values = 3.0 * jax.random.normal(jax.random.fold_in(key, 1), shape, jnp.float32)
    return jnp.clip(values, -16.0, 16.0).astype(jnp.bfloat16)


def draw_k_video(key, part):
    shape = (FRAMES, ROWS, COLS, HEADS * HEAD_DIM)
    values = jax.random.normal(jax.random.fold_in(key, 2), shape, jnp.float32)
    return jnp.clip(values, -8.0, 8.0).astype(jnp.bfloat16)


def draw_q_reg(key, part):
    shape = (REGS, HEADS * HEAD_DIM)
    values = 3.0 * jax.random.normal(jax.random.fold_in(key, 4), shape, jnp.float32)
    return jnp.clip(values, -16.0, 16.0).astype(jnp.bfloat16)


def plant(result, rng, least, top_value):
    extent = result.shape
    spot = [jax.random.randint(jax.random.fold_in(rng, axis), (), 0, extent[axis]) for axis in range(len(extent))]
    result = result.at[tuple(spot)].set(least)
    longest = extent.index(max(extent))
    spot[longest] = (spot[longest] + 1) % extent[longest]
    return result.at[tuple(spot)].set(top_value)


def levels(own_key, extent, pieces, least, top_value):
    gain = 1.0
    for dim, parts in pieces:
        heights = jax.random.uniform(jax.random.fold_in(jax.random.fold_in(own_key, 6), dim), (parts,), jnp.float32, least / len(pieces), top_value / len(pieces))
        gain = gain * jnp.repeat(jnp.exp(heights), extent[dim] // parts).reshape((-1,) + (1,) * (len(extent) - 1 - dim))
    return gain


def centred(key, extent, scale, limit, pieces=(), held_as=jnp.bfloat16):
    entries = scale * jax.random.normal(key, extent, jnp.float32)
    if pieces:
        entries = entries * levels(key, extent, pieces, -0.22, 0.18)
    return jnp.clip(entries, -limit, limit).astype(held_as)


def setup_inputs(seed: int = 0, part: int = 0) -> dict:
    splits = jax.random.split(jax.random.key(seed), 8)
    part_keys = jax.random.split(jax.random.fold_in(splits[7], part), 8)
    q_video = draw_q_video(jax.random.fold_in(jax.random.fold_in(splits[7], part), 71), part)
    k_video = draw_k_video(jax.random.fold_in(jax.random.fold_in(splits[7], part), 71), part)
    v_video = centred(part_keys[2], (FRAMES, ROWS, COLS, HEADS * HEAD_DIM), 1.0, 6.0, ((0, 4), (1, 2), (3, 2)))
    q_reg = draw_q_reg(jax.random.fold_in(jax.random.fold_in(splits[7], part), 71), part)
    k_reg = centred(part_keys[4], (REGS, HEADS * HEAD_DIM), 1.0, 6.0, ((1, 2),))
    v_reg = centred(part_keys[5], (REGS, HEADS * HEAD_DIM), 1.0, 6.0, ((1, 2),))
    nbr_mask = plant((jax.random.randint(splits[6], (N_FRAME, N_ROW, COL_TILES, NBRS), 0, 4) < 3).astype(jnp.int32), jax.random.fold_in(splits[6], 1), 0, 1)
    return dict(q_video=q_video, k_video=k_video, v_video=v_video, q_reg=q_reg, k_reg=k_reg, v_reg=v_reg, nbr_mask=nbr_mask)


def tile_view(array, grid_f, grid_r, grid_c):
    features = array.shape[-1]
    array = array.reshape(grid_f, TILE_F, grid_r, TILE_R, grid_c, TILE_C, features)
    return array.transpose(0, 2, 4, 1, 3, 5, 6).reshape(grid_f, grid_r, grid_c, TILE_F * TILE_R * TILE_C, features)


def exact_product(weights, values):
    leading = weights.astype(values.dtype)
    remainder = (weights - leading.astype(weights.dtype)).astype(values.dtype)
    first = jnp.dot(leading, values, preferred_element_type=weights.dtype)
    return first + jnp.dot(remainder, values, preferred_element_type=weights.dtype)


def reference(q_video, k_video, v_video, q_reg, k_reg, v_reg, nbr_mask):
    grid_f = FRAMES // TILE_F
    grid_r = ROWS // TILE_R
    grid_c = COL_TILES
    tile_size = TILE_F * TILE_R * TILE_C
    features = HEADS * HEAD_DIM
    score_scale = HEAD_DIM ** -0.5
    window = min(3, grid_c)
    queries = tile_view(q_video, grid_f, grid_r, grid_c)
    padding = ((1, 1), (1, 1), (0, 0), (0, 0), (0, 0))
    key_tiles = jnp.pad(tile_view(k_video, grid_f, grid_r, grid_c), padding)
    value_tiles = jnp.pad(tile_view(v_video, grid_f, grid_r, grid_c), padding)
    full_mask = jnp.concatenate([nbr_mask[..., :13], jnp.ones((grid_f, grid_r, grid_c, 1), jnp.int32), nbr_mask[..., 13:]], -1)
    offsets = jnp.arange(3, dtype=jnp.int32) - 1

    def one_tile(tile_index):
        frame_tile = tile_index // (grid_r * grid_c)
        row_tile = (tile_index // grid_c) % grid_r
        col_tile = tile_index % grid_c
        first_col = jnp.clip(col_tile - 1, 0, grid_c - window).astype(jnp.int32)
        anchor = jnp.zeros((), jnp.int32)
        start_at = (frame_tile, row_tile, first_col, anchor, anchor)
        near_keys = lax.dynamic_slice(key_tiles, start_at, (3, 3, window, tile_size, features)).reshape(9 * window * tile_size, features)
        near_values = lax.dynamic_slice(value_tiles, start_at, (3, 3, window, tile_size, features)).reshape(9 * window * tile_size, features)
        key_cols = first_col + jnp.arange(window, dtype=jnp.int32)
        offset_codes = (offsets[:, None, None] + 1) * 9 + (offsets[None, :, None] + 1) * 3 + (key_cols - col_tile + 1)[None, None, :]
        mask_row = full_mask[frame_tile, row_tile, col_tile]
        picked = jnp.sum(jnp.where(offset_codes[..., None] == jnp.arange(27, dtype=jnp.int32), mask_row, 0), axis=-1)
        frame_inside = (frame_tile + offsets >= 0) & (frame_tile + offsets < grid_f)
        row_inside = (row_tile + offsets >= 0) & (row_tile + offsets < grid_r)
        adjacent = jnp.abs(key_cols - col_tile) <= 1
        allowed = (picked == 1) & frame_inside[:, None, None] & row_inside[None, :, None] & adjacent[None, None, :]
        key_ok = jnp.concatenate([jnp.repeat(allowed.reshape(-1), tile_size, total_repeat_length=9 * window * tile_size), jnp.ones((REGS,), bool)])
        all_keys = jnp.concatenate([near_keys, k_reg], 0)
        all_values = jnp.concatenate([near_values, v_reg], 0)
        query_tile = queries[frame_tile, row_tile, col_tile]

        def one_head(head_index):
            query_head = lax.dynamic_slice_in_dim(query_tile, head_index * HEAD_DIM, HEAD_DIM, 1)
            key_head = lax.dynamic_slice_in_dim(all_keys, head_index * HEAD_DIM, HEAD_DIM, 1)
            value_head = lax.dynamic_slice_in_dim(all_values, head_index * HEAD_DIM, HEAD_DIM, 1)
            scores = jnp.dot(query_head, key_head.T, preferred_element_type=jnp.float32) * score_scale
            scores = jnp.where(key_ok[None, :], scores, -jnp.inf)
            weights = jax.nn.softmax(scores, axis=-1).astype(jnp.bfloat16)
            return jnp.dot(weights, value_head, preferred_element_type=jnp.float32).astype(jnp.bfloat16)

        return lax.map(one_head, jnp.arange(HEADS, dtype=jnp.int32))

    tiles_out = lax.map(one_tile, jnp.arange(grid_f * grid_r * grid_c, dtype=jnp.int32))
    tiles_out = tiles_out.reshape(grid_f, grid_r, grid_c, HEADS, TILE_F, TILE_R, TILE_C, HEAD_DIM)
    out_video = tiles_out.transpose(0, 4, 1, 5, 2, 6, 3, 7).reshape(FRAMES, ROWS, COLS, features)

    flat_keys = jnp.concatenate([k_video.reshape(-1, features), k_reg], 0)
    flat_values = jnp.concatenate([v_video.reshape(-1, features), v_reg], 0)

    def register_head(head_index):
        query_head = lax.dynamic_slice_in_dim(q_reg, head_index * HEAD_DIM, HEAD_DIM, 1)
        key_head = lax.dynamic_slice_in_dim(flat_keys, head_index * HEAD_DIM, HEAD_DIM, 1)
        value_head = lax.dynamic_slice_in_dim(flat_values, head_index * HEAD_DIM, HEAD_DIM, 1)
        scores = jnp.dot(query_head, key_head.T, preferred_element_type=jnp.float32) * score_scale
        weights = jax.nn.softmax(scores, axis=-1)
        return exact_product(weights, value_head)

    register_out = lax.map(register_head, jnp.arange(HEADS, dtype=jnp.int32))
    out_reg = register_out.transpose(1, 0, 2).reshape(REGS, features).astype(jnp.bfloat16)
    return out_video, out_reg
```

```python
import functools

import jax
import jax.numpy as jnp
from jax import lax
from jax.experimental import pallas as pl
from jax.experimental.pallas import tpu as pltpu
from jax.sharding import PartitionSpec as P

HEAD_DIM = 128
NEG = -1e30
SCALE = HEAD_DIM ** -0.5
LOG2E = 1.4426950408889634
MESH = pl.DeviceIdType.MESH
SLOT_DF = (0, -1, 1)


def offset_index(df, dr, dc):
    code = 9 * (df + 1) + 3 * (dr + 1) + (dc + 1)
    return code - 1 if code > 13 else code


def nt(a, b):
    return lax.dot_general(a, b, (((1,), (1,)), ((), ())), preferred_element_type=jnp.float32)


def tn(a, b):
    return lax.dot_general(a, b, (((0,), (0,)), ((), ())), preferred_element_type=jnp.float32)


def block_kernel(dims, *refs):
    (heads, tokens, columns, tile_c, col_tiles, regs, n_frame, n_row, with_regs) = dims
    peers = n_frame * n_row
    share = regs // peers
    nbrs = 0 if n_row == 1 else (1 if n_row == 2 else 2)
    if with_regs:
        (q_hbm, k_hbm, v_hbm, qr_ref, kr_ref, vr_ref, mask_ref, out_ref, outr_ref,
         qbuf, kv, bias, bias_out, s_ref, o_own, st_own, o_out, st_out, o_in, st_in,
         ld_sem, zs, zr, xs, xr, bs, br, osd, orv, sts, str_,
         r_out, rst_t, rst_out, r_in, rst_in, rs, rr) = refs
    else:
        (q_hbm, k_hbm, v_hbm, kr_ref, vr_ref, mask_ref, out_ref,
         qbuf, kv, bias, bias_out, s_ref, o_own, st_own, o_out, st_out, o_in, st_in,
         ld_sem, zs, zr, xs, xr, bs, br, osd, orv, sts, str_) = refs
    frame = lax.axis_index("frame")
    row = lax.axis_index("row")
    me = frame * n_row + row
    coef = jnp.float32(SCALE * LOG2E)

    def cols(h):
        return pl.ds(pl.multiple_of(h * HEAD_DIM, HEAD_DIM), HEAD_DIM)

    def load(h):
        return (
            pltpu.make_async_copy(k_hbm.at[:, cols(h)], kv.at[0, h, 0], ld_sem.at[0, h]),
            pltpu.make_async_copy(v_hbm.at[:, cols(h)], kv.at[0, h, 1], ld_sem.at[1, h]),
            pltpu.make_async_copy(q_hbm.at[:, cols(h)], qbuf.at[0, h], ld_sem.at[2, h]),
        )

    for h in range(heads):
        for copy in load(h):
            copy.start()

    frame_links = (
        (1, {"frame": frame + 1}, frame < n_frame - 1, 0),
        (2, {"frame": frame - 1}, frame > 0, 1),
    )
    if nbrs == 0:
        row_links = ()
    elif nbrs == 1:
        row_links = ((0, {"row": 1 - row}, None),)
    else:
        row_links = ((1, {"row": row - 1}, row > 0), (0, {"row": row + 1}, row < n_row - 1))

    def guarded(cond, fn):
        if cond is None:
            fn()
        else:
            pl.when(cond)(fn)

    barrier = pltpu.get_barrier_semaphore()
    if with_regs:
        for k in range(1, peers):
            peer = lax.rem(me + k, peers)
            pl.semaphore_signal(
                barrier, inc=1, device_id={"frame": peer // n_row, "row": lax.rem(peer, n_row)},
                device_id_type=MESH,
            )
        pl.semaphore_wait(barrier, peers - 1)
    else:
        links = [(dev, ok) for _, dev, ok, _ in frame_links] + [(dev, ok) for _, dev, ok in row_links]
        for dev, ok in links:
            guarded(ok, lambda dev=dev: pl.semaphore_signal(
                barrier, inc=1, device_id=dev, device_id_type=MESH))
        for dev, ok in links:
            guarded(ok, lambda: pl.semaphore_wait(barrier, 1))

    def kv_copy(h, link):
        slot, dev, _, i = link
        return pltpu.make_async_remote_copy(
            src_ref=kv.at[0, h], dst_ref=kv.at[slot, h], send_sem=zs.at[i, h],
            recv_sem=zr.at[slot - 1, h], device_id=dev, device_id_type=MESH)

    def q_copy(h, j):
        theirs, dev, _ = row_links[j]
        return pltpu.make_async_remote_copy(
            src_ref=qbuf.at[0, h], dst_ref=qbuf.at[1 + theirs, h], send_sem=xs.at[j, h],
            recv_sem=xr.at[theirs, h], device_id=dev, device_id_type=MESH)

    def bias_copy(j):
        theirs, dev, _ = row_links[j]
        return pltpu.make_async_remote_copy(
            src_ref=bias_out.at[j], dst_ref=bias.at[1 + theirs], send_sem=bs.at[j],
            recv_sem=br.at[theirs], device_id=dev, device_id_type=MESH)

    def o_copy(h, j):
        theirs, dev, _ = row_links[j]
        return (
            pltpu.make_async_remote_copy(
                src_ref=o_out.at[j, h], dst_ref=o_in.at[theirs, h], send_sem=osd.at[j, h],
                recv_sem=orv.at[theirs, h], device_id=dev, device_id_type=MESH),
            pltpu.make_async_remote_copy(
                src_ref=st_out.at[j, h], dst_ref=st_in.at[theirs, h], send_sem=sts.at[j, h],
                recv_sem=str_.at[theirs, h], device_id=dev, device_id_type=MESH),
        )

    for h in range(heads):
        copies = load(h)
        copies[0].wait()
        copies[1].wait()
        for link in frame_links:
            guarded(link[2], lambda link=link: kv_copy(h, link).start())
        copies[2].wait()
        for j in range(nbrs):
            guarded(row_links[j][2], lambda j=j: q_copy(h, j).start())

    lane_tile = (lax.broadcasted_iota(jnp.int32, (1, tokens), 1) % columns) // tile_c
    frame_ok = [None, (frame > 0).astype(jnp.int32), (frame < n_frame - 1).astype(jnp.int32)]
    bias[0] = jnp.zeros(bias.shape[1:], bias.dtype)
    if nbrs:
        bias_out[...] = jnp.zeros_like(bias_out)
    for target in range(1 + nbrs):
        for slot, df in enumerate(SLOT_DF):
            for tk in range(col_tiles):
                vec = jnp.full((1, tokens), NEG, jnp.float32)
                for tq in range(col_tiles):
                    dc = tk - tq
                    if abs(dc) > 1:
                        continue
                    if target == 0:
                        if df == 0 and dc == 0:
                            ok = jnp.int32(1)
                        else:
                            ok = mask_ref[0, 0, tq, offset_index(df, 0, dc)]
                    elif nbrs == 1:
                        plus, minus = offset_index(df, 1, dc), offset_index(df, -1, dc)
                        ok = mask_ref[0, 0, tq, plus + row * (minus - plus)]
                    else:
                        ok = mask_ref[0, 0, tq, offset_index(df, (-1, 1)[target - 1], dc)]
                    if frame_ok[slot] is not None:
                        ok = ok * frame_ok[slot]
                    vec = jnp.where(lane_tile == tq, (ok.astype(jnp.float32) - 1.0) * -NEG, vec)
                r = slot * col_tiles + tk
                if target == 0:
                    bias[0, r:r + 1, :] = vec
                else:
                    bias_out[target - 1, r:r + 1, :] = vec
    for j in range(nbrs):
        guarded(row_links[j][2], lambda j=j: bias_copy(j).start())

    @pl.when(frame == 0)
    def _():
        kv[1] = jnp.zeros(kv.shape[1:], kv.dtype)

    @pl.when(frame == n_frame - 1)
    def _():
        kv[2] = jnp.zeros(kv.shape[1:], kv.dtype)

    for j in range(nbrs):
        if row_links[j][2] is not None:
            @pl.when(jnp.logical_not(row_links[j][2]))
            def _():
                qbuf[1 + j] = jnp.zeros(qbuf.shape[1:], qbuf.dtype)
                bias[1 + j] = jnp.zeros(bias.shape[1:], bias.dtype)

    if with_regs:
        own_lane = lax.broadcasted_iota(jnp.int32, (1, regs), 1) // share == me
        reg_bias = jnp.where(own_lane, 0.0, NEG).astype(jnp.float32)

        def reg_head(h, carry):
            qh = qr_ref[:, cols(h)]
            s0 = nt(kv[0, h, 0], qh) * coef
            s1 = nt(kr_ref[:, cols(h)], qh) * coef + reg_bias
            m = jnp.maximum(jnp.max(s0, 0, keepdims=True), jnp.max(s1, 0, keepdims=True))
            p0 = jnp.exp2(s0 - m)
            p1 = jnp.exp2(s1 - m)
            l = jnp.sum(p0, 0, keepdims=True) + jnp.sum(p1, 0, keepdims=True)
            acc = tn(kv[0, h, 1], p0.astype(jnp.bfloat16)) + tn(vr_ref[:, cols(h)], p1.astype(jnp.bfloat16))
            r_out[:, h] = acc.T.reshape(peers, share, HEAD_DIM).astype(jnp.bfloat16)
            rst_t[pl.ds(h, 1), :] = m
            rst_t[pl.ds(heads + h, 1), :] = l
            return carry

        rst_t[...] = jnp.zeros_like(rst_t)
        lax.fori_loop(0, heads, reg_head, 0)
        rst_out[...] = rst_t[...].T.reshape(rst_out.shape)

        def reg_copy(k):
            peer = lax.rem(me + k, peers)
            dev = {"frame": peer // n_row, "row": lax.rem(peer, n_row)}
            return (
                pltpu.make_async_remote_copy(
                    src_ref=r_out.at[peer], dst_ref=r_in.at[k], send_sem=rs.at[0, k],
                    recv_sem=rr.at[0, k], device_id=dev, device_id_type=MESH),
                pltpu.make_async_remote_copy(
                    src_ref=rst_out.at[peer], dst_ref=rst_in.at[k], send_sem=rs.at[1, k],
                    recv_sem=rr.at[1, k], device_id=dev, device_id_type=MESH),
            )

        for k in range(1, peers):
            for copy in reg_copy(k):
                copy.start()

    for j in range(nbrs):
        guarded(row_links[j][2], lambda j=j: pltpu.make_async_remote_copy(
            src_ref=bias_out.at[j], dst_ref=bias.at[1 + j], send_sem=bs.at[j], recv_sem=br.at[j],
            device_id=row_links[j][1], device_id_type=MESH).wait_recv())

    lanes = (1 + nbrs) * tokens

    def video_head(h, carry):
        for j in range(nbrs):
            guarded(row_links[j][2], lambda j=j: pltpu.make_async_remote_copy(
                src_ref=qbuf.at[0, h], dst_ref=qbuf.at[1 + j, h], send_sem=xs.at[j, h],
                recv_sem=xr.at[j, h], device_id=row_links[j][1], device_id_type=MESH).wait_recv())
        qall = qbuf[:, h].reshape(lanes, HEAD_DIM)
        m = None
        for slot in range(3):
            if slot:
                there = (frame > 0) if slot == 1 else (frame < n_frame - 1)
                dev = {"frame": frame - 1} if slot == 1 else {"frame": frame + 1}
                guarded(there, lambda: pltpu.make_async_remote_copy(
                    src_ref=kv.at[0, h], dst_ref=kv.at[slot, h], send_sem=zs.at[slot - 1, h],
                    recv_sem=zr.at[slot - 1, h], device_id=dev, device_id_type=MESH).wait_recv())
            s = nt(kv[slot, h, 0], qall) * coef
            rows = bias[:, slot * col_tiles:(slot + 1) * col_tiles, :]
            rows = jnp.concatenate([rows[t] for t in range(1 + nbrs)], axis=1)
            s = s.reshape(tokens // columns, col_tiles, tile_c, lanes) + rows[None, :, None, :]
            s = s.reshape(tokens, lanes)
            s_ref[slot * tokens:(slot + 1) * tokens, :] = s
            top = jnp.max(s, 0, keepdims=True)
            m = top if m is None else jnp.maximum(m, top)
        sr = nt(kr_ref[:, cols(h)], qall[:tokens]) * coef
        m_own = jnp.maximum(m[:, :tokens], jnp.max(sr, 0, keepdims=True))
        m = jnp.concatenate([m_own, m[:, tokens:]], axis=1) if nbrs else m_own
        pr = jnp.exp2(sr - m_own)
        l = None
        o = None
        for slot in range(3):
            p = jnp.exp2(s_ref[slot * tokens:(slot + 1) * tokens, :] - m)
            total = jnp.sum(p, 0, keepdims=True)
            part = tn(kv[slot, h, 1], p.astype(jnp.bfloat16))
            l = total if l is None else l + total
            o = part if o is None else o + part
        for j in range(nbrs):
            sl = slice((1 + j) * tokens, (2 + j) * tokens)
            o_out[j, h] = o[:, sl].astype(jnp.bfloat16)
            st_out[j, h] = jnp.concatenate([m[:, sl]] * 4 + [l[:, sl]] * 4, axis=0)

            def send(j=j):
                for copy in o_copy(h, j):
                    copy.start()

            guarded(row_links[j][2], send)
        o_own[h] = o[:, :tokens] + tn(vr_ref[:, cols(h)], pr.astype(jnp.bfloat16))
        l_own = l[:, :tokens] + jnp.sum(pr, 0, keepdims=True)
        st_own[h] = jnp.concatenate([m_own] * 4 + [l_own] * 4, axis=0)
        return carry

    for j in range(nbrs):
        if row_links[j][2] is not None:
            @pl.when(jnp.logical_not(row_links[j][2]))
            def _():
                o_in[j] = jnp.zeros(o_in.shape[1:], o_in.dtype)
                st_in[j] = jnp.full(st_in.shape[1:], NEG, st_in.dtype)

    lax.fori_loop(0, heads, video_head, 0)

    def finish_head(h, carry):
        st = st_own[h]
        m, l, o = st[0:1], st[4:5], o_own[h]
        parts = []
        for j in range(nbrs):
            def arrive(j=j):
                pltpu.make_async_remote_copy(
                    src_ref=o_out.at[j, h], dst_ref=o_in.at[j, h], send_sem=osd.at[j, h],
                    recv_sem=orv.at[j, h], device_id=row_links[j][1], device_id_type=MESH).wait_recv()
                pltpu.make_async_remote_copy(
                    src_ref=st_out.at[j, h], dst_ref=st_in.at[j, h], send_sem=sts.at[j, h],
                    recv_sem=str_.at[j, h], device_id=row_links[j][1], device_id_type=MESH).wait_recv()

            guarded(row_links[j][2], arrive)
            other = st_in[j, h]
            parts.append((other[0:1], other[4:5], o_in[j, h].astype(jnp.float32)))
        joint = m
        for mj, _, _ in parts:
            joint = jnp.maximum(joint, mj)
        factor = jnp.exp2(m - joint)
        total = l * factor
        factors = []
        for mj, lj, _ in parts:
            fj = jnp.exp2(mj - joint)
            factors.append(fj)
            total = total + lj * fj
        inv = 1.0 / total
        o = o * (factor * inv)
        for fj, (_, _, oj) in zip(factors, parts):
            o = o + oj * (fj * inv)
        out_ref[:, cols(h)] = o.T.astype(jnp.bfloat16)
        return carry

    lax.fori_loop(0, heads, finish_head, 0)

    if with_regs:
        for k in range(1, peers):
            for copy in reg_copy(k):
                copy.wait_recv()
        for h in range(heads):
            ms = [rst_out[me][:, h:h + 1]] + [rst_in[k][:, h:h + 1] for k in range(1, peers)]
            ls = [rst_out[me][:, heads + h:heads + h + 1]] + [
                rst_in[k][:, heads + h:heads + h + 1] for k in range(1, peers)]
            accs = [r_out[me, h]] + [r_in[k, h] for k in range(1, peers)]
            joint = functools.reduce(jnp.maximum, ms)
            total = None
            acc = None
            for mk, lk, ak in zip(ms, ls, accs):
                f = jnp.exp2(mk - joint)
                tk, wk = lk * f, ak.astype(jnp.float32) * f
                total = tk if total is None else total + tk
                acc = wk if acc is None else acc + wk
            outr_ref[:, h * HEAD_DIM:(h + 1) * HEAD_DIM] = (acc / total).astype(jnp.bfloat16)

    def sent(h, carry):
        for link in frame_links:
            guarded(link[2], lambda link=link: kv_copy(h, link).wait_send())
        for j in range(nbrs):
            def left(j=j):
                q_copy(h, j).wait_send()
                for copy in o_copy(h, j):
                    copy.wait_send()

            guarded(row_links[j][2], left)
        return carry

    lax.fori_loop(0, heads, sent, 0)
    for j in range(nbrs):
        guarded(row_links[j][2], lambda j=j: bias_copy(j).wait_send())
    if with_regs:
        for k in range(1, peers):
            for copy in reg_copy(k):
                copy.wait_send()


def exact_product(weights, values):
    leading = weights.astype(values.dtype)
    remainder = (weights - leading.astype(weights.dtype)).astype(values.dtype)
    return jnp.einsum("hqk,khd->hqd", leading, values, preferred_element_type=jnp.float32) + jnp.einsum(
        "hqk,khd->hqd", remainder, values, preferred_element_type=jnp.float32)


def partial_softmax(queries, keys, values):
    scores = jnp.einsum("qhd,khd->hqk", queries, keys, preferred_element_type=jnp.float32) * SCALE
    top = jnp.max(scores, axis=-1)
    weights = jnp.exp(scores - top[..., None])
    return top, jnp.sum(weights, axis=-1), exact_product(weights, values)


def registers_by_reduction(q_reg, k_reg, v_reg, k_video, v_video, heads, share):
    split = lambda x: x.reshape(-1, heads, HEAD_DIM)
    start = (lax.axis_index("frame") * lax.axis_size("row") + lax.axis_index("row")) * share
    top, total, weighted = partial_softmax(split(q_reg), split(k_video), split(v_video))
    joint = lax.pmax(top, ("frame", "row"))
    factor = jnp.exp(top - joint)
    total, weighted = lax.psum((total * factor, weighted * factor[..., None]), ("frame", "row"))
    own = lambda x: lax.dynamic_slice_in_dim(x, start, share, 1)
    queries = lax.dynamic_slice_in_dim(q_reg, start, share, 0)
    top2, total2, weighted2 = partial_softmax(split(queries), split(k_reg), split(v_reg))
    top1, total1, weighted1 = own(joint), own(total), own(weighted)
    last = jnp.maximum(top1, top2)
    f1, f2 = jnp.exp(top1 - last), jnp.exp(top2 - last)
    out = (weighted1 * f1[..., None] + weighted2 * f2[..., None]) / (total1 * f1 + total2 * f2)[..., None]
    return out.transpose(1, 0, 2).reshape(share, heads * HEAD_DIM).astype(jnp.bfloat16)


def on_device(q_video, k_video, v_video, q_reg, k_reg, v_reg, nbr_mask):
    tile_f, tile_r, columns, features = q_video.shape
    col_tiles = nbr_mask.shape[2]
    tile_c = columns // col_tiles
    tokens = tile_f * tile_r * columns
    heads = features // HEAD_DIM
    regs = q_reg.shape[0]
    n_frame, n_row = lax.axis_size("frame"), lax.axis_size("row")
    peers = n_frame * n_row
    share = regs // peers
    with_regs = share % 8 == 0 and 2 * heads <= 128
    nbrs = 0 if n_row == 1 else (1 if n_row == 2 else 2)
    nslot = max(nbrs, 1)
    bias_rows = -(-3 * col_tiles // 8) * 8
    dims = (heads, tokens, columns, tile_c, col_tiles, regs, n_frame, n_row, with_regs)
    bf16, f32 = jnp.bfloat16, jnp.float32
    dma = lambda *shape: pltpu.SemaphoreType.DMA(shape)
    scratch = [
        pltpu.VMEM((1 + nbrs, heads, tokens, HEAD_DIM), bf16),
        pltpu.VMEM((3, heads, 2, tokens, HEAD_DIM), bf16),
        pltpu.VMEM((1 + nbrs, bias_rows, tokens), f32),
        pltpu.VMEM((nslot, bias_rows, tokens), f32),
        pltpu.VMEM((3 * tokens, (1 + nbrs) * tokens), f32),
        pltpu.VMEM((heads, HEAD_DIM, tokens), f32),
        pltpu.VMEM((heads, 8, tokens), f32),
        pltpu.VMEM((nslot, heads, HEAD_DIM, tokens), bf16),
        pltpu.VMEM((nslot, heads, 8, tokens), f32),
        pltpu.VMEM((nslot, heads, HEAD_DIM, tokens), bf16),
        pltpu.VMEM((nslot, heads, 8, tokens), f32),
        dma(3, heads), dma(2, heads), dma(2, heads), dma(nslot, heads), dma(nslot, heads),
        dma(nslot), dma(nslot), dma(nslot, heads), dma(nslot, heads), dma(nslot, heads), dma(nslot, heads),
    ]
    out_shape = [jax.ShapeDtypeStruct((tokens, features), bf16)]
    any_spec, vmem, smem = (pl.BlockSpec(memory_space=s) for s in (pl.ANY, pltpu.VMEM, pltpu.SMEM))
    if with_regs:
        scratch += [
            pltpu.VMEM((peers, heads, share, HEAD_DIM), bf16),
            pltpu.VMEM((128, regs), f32),
            pltpu.VMEM((peers, share, 128), f32),
            pltpu.VMEM((peers, heads, share, HEAD_DIM), bf16),
            pltpu.VMEM((peers, share, 128), f32),
            dma(2, peers), dma(2, peers),
        ]
        out_shape.append(jax.ShapeDtypeStruct((share, features), bf16))
        reg_args = (q_reg, k_reg, v_reg)
    else:
        reg_args = (k_reg, v_reg)
    flat = lambda x: x.reshape(tokens, features)
    outs = pl.pallas_call(
        functools.partial(block_kernel, dims),
        out_shape=out_shape,
        in_specs=[any_spec] * 3 + [vmem] * len(reg_args) + [smem],
        out_specs=[vmem] * len(out_shape),
        scratch_shapes=scratch,
        compiler_params=pltpu.CompilerParams(
            collective_id=0, has_side_effects=True, vmem_limit_bytes=40 * 1024 * 1024),
    )(flat(q_video), flat(k_video), flat(v_video), *reg_args, nbr_mask)
    out_video = outs[0].reshape(q_video.shape)
    if with_regs:
        out_reg = outs[1]
    else:
        out_reg = registers_by_reduction(q_reg, k_reg, v_reg, k_video, v_video, heads, share)
    return out_video, out_reg


def solution(mesh):
    video = P(("group", "frame"), "row", None, "head")
    reg = P("group", "head")
    return jax.shard_map(
        on_device,
        mesh=mesh,
        in_specs=(video, video, video, reg, reg, reg, P("frame", "row", None, None)),
        out_specs=(video, P(("group", "frame", "row"), "head")),
        check_vma=False,
    )
```

```python
import functools

import jax
import jax.numpy as jnp
from jax import lax
from jax.experimental import pallas as pl
from jax.experimental.pallas import tpu as pltpu
from jax.sharding import PartitionSpec as P

HEAD_DIM = 128
NEG = -1e30
SCALE = HEAD_DIM ** -0.5
LOG2E = 1.4426950408889634
MESH = pl.DeviceIdType.MESH
SLOT_DF = (0, -1, 1)


def offset_index(df, dr, dc):
    code = 9 * (df + 1) + 3 * (dr + 1) + (dc + 1)
    return code - 1 if code > 13 else code


def nt(a, b):
    return lax.dot_general(a, b, (((1,), (1,)), ((), ())), preferred_element_type=jnp.float32)


def tn(a, b):
    return lax.dot_general(a, b, (((0,), (0,)), ((), ())), preferred_element_type=jnp.float32)


def block_kernel(dims, *refs):
    (heads, tokens, columns, tile_c, col_tiles, regs, n_frame, n_row, with_regs) = dims
    peers = n_frame * n_row
    share = regs // peers
    nbrs = 0 if n_row == 1 else (1 if n_row == 2 else 2)
    if with_regs:
        (q_hbm, k_hbm, v_hbm, qr_hbm, kr_hbm, vr_hbm, mask_hbm, out_ref, outr_ref,
         kr_ref, vr_ref, mask_ref, ld_reg, qbuf, kv, bias, bias_out, s_ref, o_own, st_own, o_out, st_out, o_in, st_in,
         ld_sem, zs, zr, xs, xr, bs, br, osd, orv, sts, str_,
         qr_ref, r_out, rst_t, rst_out, r_in, rst_in, rs, rr) = refs
    else:
        (q_hbm, k_hbm, v_hbm, kr_hbm, vr_hbm, mask_hbm, out_ref,
         kr_ref, vr_ref, mask_ref, ld_reg, qbuf, kv, bias, bias_out, s_ref, o_own, st_own, o_out, st_out, o_in, st_in,
         ld_sem, zs, zr, xs, xr, bs, br, osd, orv, sts, str_) = refs
    frame = lax.axis_index("frame")
    row = lax.axis_index("row")
    me = frame * n_row + row
    coef = jnp.float32(SCALE * LOG2E)

    def cols(h):
        return pl.ds(pl.multiple_of(h * HEAD_DIM, HEAD_DIM), HEAD_DIM)

    def load(h):
        return (
            pltpu.make_async_copy(k_hbm.at[:, cols(h)], kv.at[0, h, 0], ld_sem.at[0, h]),
            pltpu.make_async_copy(v_hbm.at[:, cols(h)], kv.at[0, h, 1], ld_sem.at[1, h]),
            pltpu.make_async_copy(q_hbm.at[:, cols(h)], qbuf.at[0, h], ld_sem.at[2, h]),
        )

    for h in range(heads):
        for copy in load(h):
            copy.start()
        if h == 0:
            small = [(mask_hbm, mask_ref), (kr_hbm, kr_ref), (vr_hbm, vr_ref)]
            if with_regs:
                small.append((qr_hbm, qr_ref))
            small = [pltpu.make_async_copy(a, b, ld_reg.at[i]) for i, (a, b) in enumerate(small)]
            for copy in small:
                copy.start()

    frame_links = (
        (1, {"frame": frame + 1}, frame < n_frame - 1, 0),
        (2, {"frame": frame - 1}, frame > 0, 1),
    )
    if nbrs == 0:
        row_links = ()
    elif nbrs == 1:
        row_links = ((0, {"row": 1 - row}, None),)
    else:
        row_links = ((1, {"row": row - 1}, row > 0), (0, {"row": row + 1}, row < n_row - 1))

    def guarded(cond, fn):
        if cond is None:
            fn()
        else:
            pl.when(cond)(fn)

    barrier = pltpu.get_barrier_semaphore()
    if with_regs:
        for k in range(1, peers):
            peer = lax.rem(me + k, peers)
            pl.semaphore_signal(
                barrier, inc=1, device_id={"frame": peer // n_row, "row": lax.rem(peer, n_row)},
                device_id_type=MESH,
            )
        pl.semaphore_wait(barrier, peers - 1)
    else:
        links = [(dev, ok) for _, dev, ok, _ in frame_links] + [(dev, ok) for _, dev, ok in row_links]
        for dev, ok in links:
            guarded(ok, lambda dev=dev: pl.semaphore_signal(
                barrier, inc=1, device_id=dev, device_id_type=MESH))
        for dev, ok in links:
            guarded(ok, lambda: pl.semaphore_wait(barrier, 1))

    def kv_copy(h, link):
        slot, dev, _, i = link
        return pltpu.make_async_remote_copy(
            src_ref=kv.at[0, h], dst_ref=kv.at[slot, h], send_sem=zs.at[i, h],
            recv_sem=zr.at[slot - 1, h], device_id=dev, device_id_type=MESH)

    def q_copy(h, j):
        theirs, dev, _ = row_links[j]
        return pltpu.make_async_remote_copy(
            src_ref=qbuf.at[0, h], dst_ref=qbuf.at[1 + theirs, h], send_sem=xs.at[j, h],
            recv_sem=xr.at[theirs, h], device_id=dev, device_id_type=MESH)

    def bias_copy(j):
        theirs, dev, _ = row_links[j]
        return pltpu.make_async_remote_copy(
            src_ref=bias_out.at[j], dst_ref=bias.at[1 + theirs], send_sem=bs.at[j],
            recv_sem=br.at[theirs], device_id=dev, device_id_type=MESH)

    def o_copy(h, j):
        theirs, dev, _ = row_links[j]
        return (
            pltpu.make_async_remote_copy(
                src_ref=o_out.at[j, h], dst_ref=o_in.at[theirs, h], send_sem=osd.at[j, h],
                recv_sem=orv.at[theirs, h], device_id=dev, device_id_type=MESH),
            pltpu.make_async_remote_copy(
                src_ref=st_out.at[j, h], dst_ref=st_in.at[theirs, h], send_sem=sts.at[j, h],
                recv_sem=str_.at[theirs, h], device_id=dev, device_id_type=MESH),
        )

    for h in range(heads):
        copies = load(h)
        copies[0].wait()
        copies[1].wait()
        for link in frame_links:
            guarded(link[2], lambda link=link: kv_copy(h, link).start())
        copies[2].wait()
        for j in range(nbrs):
            guarded(row_links[j][2], lambda j=j: q_copy(h, j).start())

    for copy in small:
        copy.wait()

    lane_tile = (lax.broadcasted_iota(jnp.int32, (1, tokens), 1) % columns) // tile_c
    frame_ok = [None, (frame > 0).astype(jnp.int32), (frame < n_frame - 1).astype(jnp.int32)]
    bias[0] = jnp.zeros(bias.shape[1:], bias.dtype)
    if nbrs:
        bias_out[...] = jnp.zeros_like(bias_out)
    for target in range(1 + nbrs):
        for slot, df in enumerate(SLOT_DF):
            for tk in range(col_tiles):
                vec = jnp.full((1, tokens), NEG, jnp.float32)
                for tq in range(col_tiles):
                    dc = tk - tq
                    if abs(dc) > 1:
                        continue
                    if target == 0:
                        if df == 0 and dc == 0:
                            ok = jnp.int32(1)
                        else:
                            ok = mask_ref[0, 0, tq, offset_index(df, 0, dc)]
                    elif nbrs == 1:
                        plus, minus = offset_index(df, 1, dc), offset_index(df, -1, dc)
                        ok = mask_ref[0, 0, tq, plus + row * (minus - plus)]
                    else:
                        ok = mask_ref[0, 0, tq, offset_index(df, (-1, 1)[target - 1], dc)]
                    if frame_ok[slot] is not None:
                        ok = ok * frame_ok[slot]
                    vec = jnp.where(lane_tile == tq, (ok.astype(jnp.float32) - 1.0) * -NEG, vec)
                r = slot * col_tiles + tk
                if target == 0:
                    bias[0, r:r + 1, :] = vec
                else:
                    bias_out[target - 1, r:r + 1, :] = vec
    for j in range(nbrs):
        guarded(row_links[j][2], lambda j=j: bias_copy(j).start())

    @pl.when(frame == 0)
    def _():
        kv[1] = jnp.zeros(kv.shape[1:], kv.dtype)

    @pl.when(frame == n_frame - 1)
    def _():
        kv[2] = jnp.zeros(kv.shape[1:], kv.dtype)

    for j in range(nbrs):
        if row_links[j][2] is not None:
            @pl.when(jnp.logical_not(row_links[j][2]))
            def _():
                qbuf[1 + j] = jnp.zeros(qbuf.shape[1:], qbuf.dtype)
                bias[1 + j] = jnp.zeros(bias.shape[1:], bias.dtype)

    if with_regs:
        own_lane = lax.broadcasted_iota(jnp.int32, (1, regs), 1) // share == me
        reg_bias = jnp.where(own_lane, 0.0, NEG).astype(jnp.float32)

        def reg_head(h, carry):
            qh = qr_ref[:, cols(h)]
            s0 = nt(kv[0, h, 0], qh) * coef
            s1 = nt(kr_ref[:, cols(h)], qh) * coef + reg_bias
            m = jnp.maximum(jnp.max(s0, 0, keepdims=True), jnp.max(s1, 0, keepdims=True))
            p0 = jnp.exp2(s0 - m)
            p1 = jnp.exp2(s1 - m)
            l = jnp.sum(p0, 0, keepdims=True) + jnp.sum(p1, 0, keepdims=True)
            acc = tn(kv[0, h, 1], p0.astype(jnp.bfloat16)) + tn(vr_ref[:, cols(h)], p1.astype(jnp.bfloat16))
            r_out[:, h] = acc.T.reshape(peers, share, HEAD_DIM).astype(jnp.bfloat16)
            rst_t[pl.ds(h, 1), :] = m
            rst_t[pl.ds(heads + h, 1), :] = l
            return carry

        rst_t[...] = jnp.zeros_like(rst_t)
        lax.fori_loop(0, heads, reg_head, 0)
        rst_out[...] = rst_t[...].T.reshape(rst_out.shape)

        def reg_copy(k):
            peer = lax.rem(me + k, peers)
            dev = {"frame": peer // n_row, "row": lax.rem(peer, n_row)}
            return (
                pltpu.make_async_remote_copy(
                    src_ref=r_out.at[peer], dst_ref=r_in.at[k], send_sem=rs.at[0, k],
                    recv_sem=rr.at[0, k], device_id=dev, device_id_type=MESH),
                pltpu.make_async_remote_copy(
                    src_ref=rst_out.at[peer], dst_ref=rst_in.at[k], send_sem=rs.at[1, k],
                    recv_sem=rr.at[1, k], device_id=dev, device_id_type=MESH),
            )

        for k in range(1, peers):
            for copy in reg_copy(k):
                copy.start()

    for j in range(nbrs):
        guarded(row_links[j][2], lambda j=j: pltpu.make_async_remote_copy(
            src_ref=bias_out.at[j], dst_ref=bias.at[1 + j], send_sem=bs.at[j], recv_sem=br.at[j],
            device_id=row_links[j][1], device_id_type=MESH).wait_recv())

    lanes = (1 + nbrs) * tokens

    def video_head(h, carry):
        for j in range(nbrs):
            guarded(row_links[j][2], lambda j=j: pltpu.make_async_remote_copy(
                src_ref=qbuf.at[0, h], dst_ref=qbuf.at[1 + j, h], send_sem=xs.at[j, h],
                recv_sem=xr.at[j, h], device_id=row_links[j][1], device_id_type=MESH).wait_recv())
        qall = qbuf[:, h].reshape(lanes, HEAD_DIM)
        m = None
        for slot in range(3):
            if slot:
                there = (frame > 0) if slot == 1 else (frame < n_frame - 1)
                dev = {"frame": frame - 1} if slot == 1 else {"frame": frame + 1}
                guarded(there, lambda: pltpu.make_async_remote_copy(
                    src_ref=kv.at[0, h], dst_ref=kv.at[slot, h], send_sem=zs.at[slot - 1, h],
                    recv_sem=zr.at[slot - 1, h], device_id=dev, device_id_type=MESH).wait_recv())
            s = nt(kv[slot, h, 0], qall) * coef
            rows = bias[:, slot * col_tiles:(slot + 1) * col_tiles, :]
            rows = jnp.concatenate([rows[t] for t in range(1 + nbrs)], axis=1)
            s = s.reshape(tokens // columns, col_tiles, tile_c, lanes) + rows[None, :, None, :]
            s = s.reshape(tokens, lanes)
            s_ref[slot * tokens:(slot + 1) * tokens, :] = s
            top = jnp.max(s, 0, keepdims=True)
            m = top if m is None else jnp.maximum(m, top)
        sr = nt(kr_ref[:, cols(h)], qall[:tokens]) * coef
        m_own = jnp.maximum(m[:, :tokens], jnp.max(sr, 0, keepdims=True))
        m = jnp.concatenate([m_own, m[:, tokens:]], axis=1) if nbrs else m_own
        pr = jnp.exp2(sr - m_own)
        l = None
        o = None
        for slot in range(3):
            p = jnp.exp2(s_ref[slot * tokens:(slot + 1) * tokens, :] - m)
            total = jnp.sum(p, 0, keepdims=True)
            part = tn(kv[slot, h, 1], p.astype(jnp.bfloat16))
            l = total if l is None else l + total
            o = part if o is None else o + part
        for j in range(nbrs):
            sl = slice((1 + j) * tokens, (2 + j) * tokens)
            o_out[j, h] = o[:, sl].astype(jnp.bfloat16)
            st_out[j, h] = jnp.concatenate([m[:, sl]] * 4 + [l[:, sl]] * 4, axis=0)

            def send(j=j):
                for copy in o_copy(h, j):
                    copy.start()

            guarded(row_links[j][2], send)
        o_own[h] = o[:, :tokens] + tn(vr_ref[:, cols(h)], pr.astype(jnp.bfloat16))
        l_own = l[:, :tokens] + jnp.sum(pr, 0, keepdims=True)
        st_own[h] = jnp.concatenate([m_own] * 4 + [l_own] * 4, axis=0)
        return carry

    for j in range(nbrs):
        if row_links[j][2] is not None:
            @pl.when(jnp.logical_not(row_links[j][2]))
            def _():
                o_in[j] = jnp.zeros(o_in.shape[1:], o_in.dtype)
                st_in[j] = jnp.full(st_in.shape[1:], NEG, st_in.dtype)

    lax.fori_loop(0, heads, video_head, 0)

    def finish_head(h, carry):
        st = st_own[h]
        m, l, o = st[0:1], st[4:5], o_own[h]
        parts = []
        for j in range(nbrs):
            def arrive(j=j):
                pltpu.make_async_remote_copy(
                    src_ref=o_out.at[j, h], dst_ref=o_in.at[j, h], send_sem=osd.at[j, h],
                    recv_sem=orv.at[j, h], device_id=row_links[j][1], device_id_type=MESH).wait_recv()
                pltpu.make_async_remote_copy(
                    src_ref=st_out.at[j, h], dst_ref=st_in.at[j, h], send_sem=sts.at[j, h],
                    recv_sem=str_.at[j, h], device_id=row_links[j][1], device_id_type=MESH).wait_recv()

            guarded(row_links[j][2], arrive)
            other = st_in[j, h]
            parts.append((other[0:1], other[4:5], o_in[j, h].astype(jnp.float32)))
        joint = m
        for mj, _, _ in parts:
            joint = jnp.maximum(joint, mj)
        factor = jnp.exp2(m - joint)
        total = l * factor
        factors = []
        for mj, lj, _ in parts:
            fj = jnp.exp2(mj - joint)
            factors.append(fj)
            total = total + lj * fj
        inv = 1.0 / total
        o = o * (factor * inv)
        for fj, (_, _, oj) in zip(factors, parts):
            o = o + oj * (fj * inv)
        out_ref[:, cols(h)] = o.T.astype(jnp.bfloat16)
        return carry

    if with_regs:
        for k in range(1, peers):
            for copy in reg_copy(k):
                copy.wait_recv()
        for h in range(heads):
            ms = [rst_out[me][:, h:h + 1]] + [rst_in[k][:, h:h + 1] for k in range(1, peers)]
            ls = [rst_out[me][:, heads + h:heads + h + 1]] + [
                rst_in[k][:, heads + h:heads + h + 1] for k in range(1, peers)]
            accs = [r_out[me, h]] + [r_in[k, h] for k in range(1, peers)]
            joint = functools.reduce(jnp.maximum, ms)
            total = None
            acc = None
            for mk, lk, ak in zip(ms, ls, accs):
                f = jnp.exp2(mk - joint)
                tk, wk = lk * f, ak.astype(jnp.float32) * f
                total = tk if total is None else total + tk
                acc = wk if acc is None else acc + wk
            outr_ref[:, h * HEAD_DIM:(h + 1) * HEAD_DIM] = (acc / total).astype(jnp.bfloat16)

    lax.fori_loop(0, heads, finish_head, 0)

    def sent(h, carry):
        for link in frame_links:
            guarded(link[2], lambda link=link: kv_copy(h, link).wait_send())
        for j in range(nbrs):
            def left(j=j):
                q_copy(h, j).wait_send()
                for copy in o_copy(h, j):
                    copy.wait_send()

            guarded(row_links[j][2], left)
        return carry

    lax.fori_loop(0, heads, sent, 0)
    for j in range(nbrs):
        guarded(row_links[j][2], lambda j=j: bias_copy(j).wait_send())
    if with_regs:
        for k in range(1, peers):
            for copy in reg_copy(k):
                copy.wait_send()


def exact_product(weights, values):
    leading = weights.astype(values.dtype)
    remainder = (weights - leading.astype(weights.dtype)).astype(values.dtype)
    return jnp.einsum("hqk,khd->hqd", leading, values, preferred_element_type=jnp.float32) + jnp.einsum(
        "hqk,khd->hqd", remainder, values, preferred_element_type=jnp.float32)


def partial_softmax(queries, keys, values):
    scores = jnp.einsum("qhd,khd->hqk", queries, keys, preferred_element_type=jnp.float32) * SCALE
    top = jnp.max(scores, axis=-1)
    weights = jnp.exp(scores - top[..., None])
    return top, jnp.sum(weights, axis=-1), exact_product(weights, values)


def registers_by_reduction(q_reg, k_reg, v_reg, k_video, v_video, heads, share):
    split = lambda x: x.reshape(-1, heads, HEAD_DIM)
    start = (lax.axis_index("frame") * lax.axis_size("row") + lax.axis_index("row")) * share
    top, total, weighted = partial_softmax(split(q_reg), split(k_video), split(v_video))
    joint = lax.pmax(top, ("frame", "row"))
    factor = jnp.exp(top - joint)
    total, weighted = lax.psum((total * factor, weighted * factor[..., None]), ("frame", "row"))
    own = lambda x: lax.dynamic_slice_in_dim(x, start, share, 1)
    queries = lax.dynamic_slice_in_dim(q_reg, start, share, 0)
    top2, total2, weighted2 = partial_softmax(split(queries), split(k_reg), split(v_reg))
    top1, total1, weighted1 = own(joint), own(total), own(weighted)
    last = jnp.maximum(top1, top2)
    f1, f2 = jnp.exp(top1 - last), jnp.exp(top2 - last)
    out = (weighted1 * f1[..., None] + weighted2 * f2[..., None]) / (total1 * f1 + total2 * f2)[..., None]
    return out.transpose(1, 0, 2).reshape(share, heads * HEAD_DIM).astype(jnp.bfloat16)


def on_device(q_video, k_video, v_video, q_reg, k_reg, v_reg, nbr_mask):
    tile_f, tile_r, columns, features = q_video.shape
    col_tiles = nbr_mask.shape[2]
    tile_c = columns // col_tiles
    tokens = tile_f * tile_r * columns
    heads = features // HEAD_DIM
    regs = q_reg.shape[0]
    n_frame, n_row = lax.axis_size("frame"), lax.axis_size("row")
    peers = n_frame * n_row
    share = regs // peers
    with_regs = share % 8 == 0 and 2 * heads <= 128
    nbrs = 0 if n_row == 1 else (1 if n_row == 2 else 2)
    nslot = max(nbrs, 1)
    bias_rows = -(-3 * col_tiles // 8) * 8
    dims = (heads, tokens, columns, tile_c, col_tiles, regs, n_frame, n_row, with_regs)
    bf16, f32 = jnp.bfloat16, jnp.float32
    dma = lambda *shape: pltpu.SemaphoreType.DMA(shape)
    scratch = [
        pltpu.VMEM((regs, features), bf16), pltpu.VMEM((regs, features), bf16),
        pltpu.SMEM(nbr_mask.shape, jnp.int32), dma(4),
        pltpu.VMEM((1 + nbrs, heads, tokens, HEAD_DIM), bf16),
        pltpu.VMEM((3, heads, 2, tokens, HEAD_DIM), bf16),
        pltpu.VMEM((1 + nbrs, bias_rows, tokens), f32),
        pltpu.VMEM((nslot, bias_rows, tokens), f32),
        pltpu.VMEM((3 * tokens, (1 + nbrs) * tokens), f32),
        pltpu.VMEM((heads, HEAD_DIM, tokens), f32),
        pltpu.VMEM((heads, 8, tokens), f32),
        pltpu.VMEM((nslot, heads, HEAD_DIM, tokens), bf16),
        pltpu.VMEM((nslot, heads, 8, tokens), f32),
        pltpu.VMEM((nslot, heads, HEAD_DIM, tokens), bf16),
        pltpu.VMEM((nslot, heads, 8, tokens), f32),
        dma(3, heads), dma(2, heads), dma(2, heads), dma(nslot, heads), dma(nslot, heads),
        dma(nslot), dma(nslot), dma(nslot, heads), dma(nslot, heads), dma(nslot, heads), dma(nslot, heads),
    ]
    out_shape = [jax.ShapeDtypeStruct((tokens, features), bf16)]
    hbm, vmem = (pl.BlockSpec(memory_space=s) for s in (pltpu.HBM, pltpu.VMEM))
    if with_regs:
        scratch += [
            pltpu.VMEM((regs, features), bf16),
            pltpu.VMEM((peers, heads, share, HEAD_DIM), bf16),
            pltpu.VMEM((128, regs), f32),
            pltpu.VMEM((peers, share, 128), f32),
            pltpu.VMEM((peers, heads, share, HEAD_DIM), bf16),
            pltpu.VMEM((peers, share, 128), f32),
            dma(2, peers), dma(2, peers),
        ]
        out_shape.append(jax.ShapeDtypeStruct((share, features), bf16))
        reg_args = (q_reg, k_reg, v_reg)
    else:
        reg_args = (k_reg, v_reg)
    flat = lambda x: x.reshape(tokens, features)
    outs = pl.pallas_call(
        functools.partial(block_kernel, dims),
        out_shape=out_shape,
        in_specs=[hbm] * (4 + len(reg_args)),
        out_specs=[vmem] * len(out_shape),
        scratch_shapes=scratch,
        compiler_params=pltpu.CompilerParams(
            collective_id=0, has_side_effects=True, vmem_limit_bytes=63 * 1024 * 1024),
    )(flat(q_video), flat(k_video), flat(v_video), *reg_args, nbr_mask)
    out_video = outs[0].reshape(q_video.shape)
    if with_regs:
        out_reg = outs[1]
    else:
        out_reg = registers_by_reduction(q_reg, k_reg, v_reg, k_video, v_video, heads, share)
    return out_video, out_reg


def solution(mesh):
    video = P(("group", "frame"), "row", None, "head")
    reg = P("group", "head")
    return jax.shard_map(
        on_device,
        mesh=mesh,
        in_specs=(video, video, video, reg, reg, reg, P("frame", "row", None, None)),
        out_specs=(video, P(("group", "frame", "row"), "head")),
        check_vma=False,
    )
```

```python
import functools

import jax
import jax.numpy as jnp
from jax import lax
from jax.experimental import pallas as pl
from jax.experimental.pallas import tpu as pltpu
from jax.sharding import PartitionSpec as P

HEAD_DIM = 128
NEG = -1e30
SCALE = HEAD_DIM ** -0.5
LOG2E = 1.4426950408889634
MESH = pl.DeviceIdType.MESH
SLOT_DF = (0, -1, 1)


def offset_index(df, dr, dc):
    code = 9 * (df + 1) + 3 * (dr + 1) + (dc + 1)
    return code - 1 if code > 13 else code


def nt(a, b):
    return lax.dot_general(a, b, (((1,), (1,)), ((), ())), preferred_element_type=jnp.float32)


def tn(a, b):
    return lax.dot_general(a, b, (((0,), (0,)), ((), ())), preferred_element_type=jnp.float32)


def block_kernel(dims, *refs):
    (heads, tokens, columns, tile_c, col_tiles, regs, n_frame, n_row, with_regs) = dims
    peers = n_frame * n_row
    share = regs // peers
    nbrs = 0 if n_row == 1 else (1 if n_row == 2 else 2)
    if with_regs:
        (q_hbm, k_hbm, v_hbm, qr_hbm, kr_hbm, vr_hbm, mask_hbm, out_ref, outr_ref,
         kr_ref, vr_ref, mask_ref, ld_reg, qbuf, kv, bias, bias_out, s_ref, o_own, st_own, o_out, st_out, o_in, st_in,
         ld_sem, zs, zr, xs, xr, bs, br, osd, orv, sts, str_,
         qr_ref, r_out, rst_t, rst_out, r_in, rst_in, rs, rr) = refs
    else:
        (q_hbm, k_hbm, v_hbm, kr_hbm, vr_hbm, mask_hbm, out_ref,
         kr_ref, vr_ref, mask_ref, ld_reg, qbuf, kv, bias, bias_out, s_ref, o_own, st_own, o_out, st_out, o_in, st_in,
         ld_sem, zs, zr, xs, xr, bs, br, osd, orv, sts, str_) = refs
    frame = lax.axis_index("frame")
    row = lax.axis_index("row")
    me = frame * n_row + row
    coef = jnp.float32(SCALE * LOG2E)

    def cols(h):
        return pl.ds(pl.multiple_of(h * HEAD_DIM, HEAD_DIM), HEAD_DIM)

    def load(h):
        return (
            pltpu.make_async_copy(k_hbm.at[:, cols(h)], kv.at[0, h, 0], ld_sem.at[0, h]),
            pltpu.make_async_copy(v_hbm.at[:, cols(h)], kv.at[0, h, 1], ld_sem.at[1, h]),
            pltpu.make_async_copy(q_hbm.at[:, cols(h)], qbuf.at[0, h], ld_sem.at[2, h]),
        )

    for h in range(heads):
        for copy in load(h):
            copy.start()
        if h == 0:
            small = [(mask_hbm, mask_ref), (kr_hbm, kr_ref), (vr_hbm, vr_ref)]
            if with_regs:
                small.append((qr_hbm, qr_ref))
            small = [pltpu.make_async_copy(a, b, ld_reg.at[i]) for i, (a, b) in enumerate(small)]
            for copy in small:
                copy.start()

    frame_links = (
        (1, {"frame": frame + 1}, frame < n_frame - 1, 0),
        (2, {"frame": frame - 1}, frame > 0, 1),
    )
    if nbrs == 0:
        row_links = ()
    elif nbrs == 1:
        row_links = ((0, {"row": 1 - row}, None),)
    else:
        row_links = ((1, {"row": row - 1}, row > 0), (0, {"row": row + 1}, row < n_row - 1))

    def guarded(cond, fn):
        if cond is None:
            fn()
        else:
            pl.when(cond)(fn)

    barrier = pltpu.get_barrier_semaphore()
    if with_regs:
        for k in range(1, peers):
            peer = lax.rem(me + k, peers)
            pl.semaphore_signal(
                barrier, inc=1, device_id={"frame": peer // n_row, "row": lax.rem(peer, n_row)},
                device_id_type=MESH,
            )
        pl.semaphore_wait(barrier, peers - 1)
    else:
        links = [(dev, ok) for _, dev, ok, _ in frame_links] + [(dev, ok) for _, dev, ok in row_links]
        for dev, ok in links:
            guarded(ok, lambda dev=dev: pl.semaphore_signal(
                barrier, inc=1, device_id=dev, device_id_type=MESH))
        for dev, ok in links:
            guarded(ok, lambda: pl.semaphore_wait(barrier, 1))

    def kv_copy(h, link):
        slot, dev, _, i = link
        return pltpu.make_async_remote_copy(
            src_ref=kv.at[0, h], dst_ref=kv.at[slot, h], send_sem=zs.at[i, h],
            recv_sem=zr.at[slot - 1, h], device_id=dev, device_id_type=MESH)

    def q_copy(h, j):
        theirs, dev, _ = row_links[j]
        return pltpu.make_async_remote_copy(
            src_ref=qbuf.at[0, h], dst_ref=qbuf.at[1 + theirs, h], send_sem=xs.at[j, h],
            recv_sem=xr.at[theirs, h], device_id=dev, device_id_type=MESH)

    def bias_copy(j):
        theirs, dev, _ = row_links[j]
        return pltpu.make_async_remote_copy(
            src_ref=bias_out.at[j], dst_ref=bias.at[1 + theirs], send_sem=bs.at[j],
            recv_sem=br.at[theirs], device_id=dev, device_id_type=MESH)

    def o_copy(h, j):
        theirs, dev, _ = row_links[j]
        return (
            pltpu.make_async_remote_copy(
                src_ref=o_out.at[j, h], dst_ref=o_in.at[theirs, h], send_sem=osd.at[j, h],
                recv_sem=orv.at[theirs, h], device_id=dev, device_id_type=MESH),
            pltpu.make_async_remote_copy(
                src_ref=st_out.at[j, h], dst_ref=st_in.at[theirs, h], send_sem=sts.at[j, h],
                recv_sem=str_.at[theirs, h], device_id=dev, device_id_type=MESH),
        )

    for h in range(heads):
        copies = load(h)
        copies[0].wait()
        copies[1].wait()
        for link in frame_links:
            guarded(link[2], lambda link=link: kv_copy(h, link).start())
        copies[2].wait()
        for j in range(nbrs):
            guarded(row_links[j][2], lambda j=j: q_copy(h, j).start())

    for copy in small:
        copy.wait()

    lane_tile = (lax.broadcasted_iota(jnp.int32, (1, tokens), 1) % columns) // tile_c
    frame_ok = [None, (frame > 0).astype(jnp.int32), (frame < n_frame - 1).astype(jnp.int32)]
    bias[0] = jnp.zeros(bias.shape[1:], bias.dtype)
    if nbrs:
        bias_out[...] = jnp.zeros_like(bias_out)
    for target in range(1 + nbrs):
        for slot, df in enumerate(SLOT_DF):
            for tk in range(col_tiles):
                vec = jnp.full((1, tokens), NEG, jnp.float32)
                for tq in range(col_tiles):
                    dc = tk - tq
                    if abs(dc) > 1:
                        continue
                    if target == 0:
                        if df == 0 and dc == 0:
                            ok = jnp.int32(1)
                        else:
                            ok = mask_ref[0, 0, tq, offset_index(df, 0, dc)]
                    elif nbrs == 1:
                        plus, minus = offset_index(df, 1, dc), offset_index(df, -1, dc)
                        ok = mask_ref[0, 0, tq, plus + row * (minus - plus)]
                    else:
                        ok = mask_ref[0, 0, tq, offset_index(df, (-1, 1)[target - 1], dc)]
                    if frame_ok[slot] is not None:
                        ok = ok * frame_ok[slot]
                    vec = jnp.where(lane_tile == tq, (ok.astype(jnp.float32) - 1.0) * -NEG, vec)
                r = slot * col_tiles + tk
                if target == 0:
                    bias[0, r:r + 1, :] = vec
                else:
                    bias_out[target - 1, r:r + 1, :] = vec
    for j in range(nbrs):
        guarded(row_links[j][2], lambda j=j: bias_copy(j).start())

    @pl.when(frame == 0)
    def _():
        kv[1] = jnp.zeros(kv.shape[1:], kv.dtype)

    @pl.when(frame == n_frame - 1)
    def _():
        kv[2] = jnp.zeros(kv.shape[1:], kv.dtype)

    for j in range(nbrs):
        if row_links[j][2] is not None:
            @pl.when(jnp.logical_not(row_links[j][2]))
            def _():
                qbuf[1 + j] = jnp.zeros(qbuf.shape[1:], qbuf.dtype)
                bias[1 + j] = jnp.zeros(bias.shape[1:], bias.dtype)

    if with_regs:
        own_lane = lax.broadcasted_iota(jnp.int32, (1, regs), 1) // share == me
        reg_bias = jnp.where(own_lane, 0.0, NEG).astype(jnp.float32)

        def reg_head(h, carry):
            qh = qr_ref[:, cols(h)]
            s0 = nt(kv[0, h, 0], qh) * coef
            s1 = nt(kr_ref[:, cols(h)], qh) * coef + reg_bias
            m = jnp.maximum(jnp.max(s0, 0, keepdims=True), jnp.max(s1, 0, keepdims=True))
            p0 = jnp.exp2(s0 - m)
            p1 = jnp.exp2(s1 - m)
            l = jnp.sum(p0, 0, keepdims=True) + jnp.sum(p1, 0, keepdims=True)
            acc = tn(kv[0, h, 1], p0.astype(jnp.bfloat16)) + tn(vr_ref[:, cols(h)], p1.astype(jnp.bfloat16))
            r_out[:, h] = acc.T.reshape(peers, share, HEAD_DIM).astype(jnp.bfloat16)
            rst_t[pl.ds(h, 1), :] = m
            rst_t[pl.ds(heads + h, 1), :] = l
            return carry

        rst_t[...] = jnp.zeros_like(rst_t)
        lax.fori_loop(0, heads, reg_head, 0)
        rst_out[...] = rst_t[...].T.reshape(rst_out.shape)

        def reg_copy(k):
            peer = lax.rem(me + k, peers)
            dev = {"frame": peer // n_row, "row": lax.rem(peer, n_row)}
            return (
                pltpu.make_async_remote_copy(
                    src_ref=r_out.at[peer], dst_ref=r_in.at[k], send_sem=rs.at[0, k],
                    recv_sem=rr.at[0, k], device_id=dev, device_id_type=MESH),
                pltpu.make_async_remote_copy(
                    src_ref=rst_out.at[peer], dst_ref=rst_in.at[k], send_sem=rs.at[1, k],
                    recv_sem=rr.at[1, k], device_id=dev, device_id_type=MESH),
            )

        for k in range(1, peers):
            for copy in reg_copy(k):
                copy.start()

    for j in range(nbrs):
        guarded(row_links[j][2], lambda j=j: pltpu.make_async_remote_copy(
            src_ref=bias_out.at[j], dst_ref=bias.at[1 + j], send_sem=bs.at[j], recv_sem=br.at[j],
            device_id=row_links[j][1], device_id_type=MESH).wait_recv())

    lanes = (1 + nbrs) * tokens

    def video_head(h, carry):
        for j in range(nbrs):
            guarded(row_links[j][2], lambda j=j: pltpu.make_async_remote_copy(
                src_ref=qbuf.at[0, h], dst_ref=qbuf.at[1 + j, h], send_sem=xs.at[j, h],
                recv_sem=xr.at[j, h], device_id=row_links[j][1], device_id_type=MESH).wait_recv())
        qall = qbuf[:, h].reshape(lanes, HEAD_DIM)
        m = None
        for slot in range(3):
            if slot:
                there = (frame > 0) if slot == 1 else (frame < n_frame - 1)
                dev = {"frame": frame - 1} if slot == 1 else {"frame": frame + 1}
                guarded(there, lambda: pltpu.make_async_remote_copy(
                    src_ref=kv.at[0, h], dst_ref=kv.at[slot, h], send_sem=zs.at[slot - 1, h],
                    recv_sem=zr.at[slot - 1, h], device_id=dev, device_id_type=MESH).wait_recv())
            s = nt(kv[slot, h, 0], qall) * coef
            rows = bias[:, slot * col_tiles:(slot + 1) * col_tiles, :]
            rows = jnp.concatenate([rows[t] for t in range(1 + nbrs)], axis=1)
            s = s.reshape(tokens // columns, col_tiles, tile_c, lanes) + rows[None, :, None, :]
            s = s.reshape(tokens, lanes)
            s_ref[slot * tokens:(slot + 1) * tokens, :] = s
            top = jnp.max(s, 0, keepdims=True)
            m = top if m is None else jnp.maximum(m, top)
        sr = nt(kr_ref[:, cols(h)], qall[:tokens]) * coef
        m_own = jnp.maximum(m[:, :tokens], jnp.max(sr, 0, keepdims=True))
        m = jnp.concatenate([m_own, m[:, tokens:]], axis=1) if nbrs else m_own
        pr = jnp.exp2(sr - m_own)
        l = None
        o = None
        for slot in range(3):
            p = jnp.exp2(s_ref[slot * tokens:(slot + 1) * tokens, :] - m)
            total = jnp.sum(p, 0, keepdims=True)
            part = tn(kv[slot, h, 1], p.astype(jnp.bfloat16))
            l = total if l is None else l + total
            o = part if o is None else o + part
        for j in range(nbrs):
            sl = slice((1 + j) * tokens, (2 + j) * tokens)
            o_out[j, h] = o[:, sl].astype(jnp.bfloat16)
            st_out[j, h] = jnp.concatenate([m[:, sl]] * 4 + [l[:, sl]] * 4, axis=0)

            def send(j=j):
                for copy in o_copy(h, j):
                    copy.start()

            guarded(row_links[j][2], send)
        o_own[h] = o[:, :tokens] + tn(vr_ref[:, cols(h)], pr.astype(jnp.bfloat16))
        l_own = l[:, :tokens] + jnp.sum(pr, 0, keepdims=True)
        st_own[h] = jnp.concatenate([m_own] * 4 + [l_own] * 4, axis=0)
        return carry

    for j in range(nbrs):
        if row_links[j][2] is not None:
            @pl.when(jnp.logical_not(row_links[j][2]))
            def _():
                o_in[j] = jnp.zeros(o_in.shape[1:], o_in.dtype)
                st_in[j] = jnp.full(st_in.shape[1:], NEG, st_in.dtype)

    lax.fori_loop(0, heads, video_head, 0)

    def finish_head(h, carry):
        st = st_own[h]
        m, l, o = st[0:1], st[4:5], o_own[h]
        parts = []
        for j in range(nbrs):
            def arrive(j=j):
                pltpu.make_async_remote_copy(
                    src_ref=o_out.at[j, h], dst_ref=o_in.at[j, h], send_sem=osd.at[j, h],
                    recv_sem=orv.at[j, h], device_id=row_links[j][1], device_id_type=MESH).wait_recv()
                pltpu.make_async_remote_copy(
                    src_ref=st_out.at[j, h], dst_ref=st_in.at[j, h], send_sem=sts.at[j, h],
                    recv_sem=str_.at[j, h], device_id=row_links[j][1], device_id_type=MESH).wait_recv()

            guarded(row_links[j][2], arrive)
            other = st_in[j, h]
            parts.append((other[0:1], other[4:5], o_in[j, h].astype(jnp.float32)))
        joint = m
        for mj, _, _ in parts:
            joint = jnp.maximum(joint, mj)
        factor = jnp.exp2(m - joint)
        total = l * factor
        factors = []
        for mj, lj, _ in parts:
            fj = jnp.exp2(mj - joint)
            factors.append(fj)
            total = total + lj * fj
        inv = 1.0 / total
        o = o * (factor * inv)
        for fj, (_, _, oj) in zip(factors, parts):
            o = o + oj * (fj * inv)
        out_ref[:, cols(h)] = o.T.astype(jnp.bfloat16)
        return carry

    if with_regs:
        for k in range(1, peers):
            for copy in reg_copy(k):
                copy.wait_recv()
        for h in range(heads):
            ms = [rst_out[me][:, h:h + 1]] + [rst_in[k][:, h:h + 1] for k in range(1, peers)]
            ls = [rst_out[me][:, heads + h:heads + h + 1]] + [
                rst_in[k][:, heads + h:heads + h + 1] for k in range(1, peers)]
            accs = [r_out[me, h]] + [r_in[k, h] for k in range(1, peers)]
            joint = functools.reduce(jnp.maximum, ms)
            total = None
            acc = None
            for mk, lk, ak in zip(ms, ls, accs):
                f = jnp.exp2(mk - joint)
                tk, wk = lk * f, ak.astype(jnp.float32) * f
                total = tk if total is None else total + tk
                acc = wk if acc is None else acc + wk
            outr_ref[:, h * HEAD_DIM:(h + 1) * HEAD_DIM] = (acc / total).astype(jnp.bfloat16)

    lax.fori_loop(0, heads, finish_head, 0)

    def sent(h, carry):
        for link in frame_links:
            guarded(link[2], lambda link=link: kv_copy(h, link).wait_send())
        for j in range(nbrs):
            def left(j=j):
                q_copy(h, j).wait_send()
                for copy in o_copy(h, j):
                    copy.wait_send()

            guarded(row_links[j][2], left)
        return carry

    lax.fori_loop(0, heads, sent, 0)
    for j in range(nbrs):
        guarded(row_links[j][2], lambda j=j: bias_copy(j).wait_send())
    if with_regs:
        for k in range(1, peers):
            for copy in reg_copy(k):
                copy.wait_send()


def exact_product(weights, values):
    leading = weights.astype(values.dtype)
    remainder = (weights - leading.astype(weights.dtype)).astype(values.dtype)
    return jnp.einsum("hqk,khd->hqd", leading, values, preferred_element_type=jnp.float32) + jnp.einsum(
        "hqk,khd->hqd", remainder, values, preferred_element_type=jnp.float32)


def partial_softmax(queries, keys, values):
    scores = jnp.einsum("qhd,khd->hqk", queries, keys, preferred_element_type=jnp.float32) * SCALE
    top = jnp.max(scores, axis=-1)
    weights = jnp.exp(scores - top[..., None])
    return top, jnp.sum(weights, axis=-1), exact_product(weights, values)


def registers_by_reduction(q_reg, k_reg, v_reg, k_video, v_video, heads, share):
    split = lambda x: x.reshape(-1, heads, HEAD_DIM)
    start = (lax.axis_index("frame") * lax.axis_size("row") + lax.axis_index("row")) * share
    top, total, weighted = partial_softmax(split(q_reg), split(k_video), split(v_video))
    joint = lax.pmax(top, ("frame", "row"))
    factor = jnp.exp(top - joint)
    total, weighted = lax.psum((total * factor, weighted * factor[..., None]), ("frame", "row"))
    own = lambda x: lax.dynamic_slice_in_dim(x, start, share, 1)
    queries = lax.dynamic_slice_in_dim(q_reg, start, share, 0)
    top2, total2, weighted2 = partial_softmax(split(queries), split(k_reg), split(v_reg))
    top1, total1, weighted1 = own(joint), own(total), own(weighted)
    last = jnp.maximum(top1, top2)
    f1, f2 = jnp.exp(top1 - last), jnp.exp(top2 - last)
    out = (weighted1 * f1[..., None] + weighted2 * f2[..., None]) / (total1 * f1 + total2 * f2)[..., None]
    return out.transpose(1, 0, 2).reshape(share, heads * HEAD_DIM).astype(jnp.bfloat16)


def on_device(q_video, k_video, v_video, q_reg, k_reg, v_reg, nbr_mask):
    tile_f, tile_r, columns, features = q_video.shape
    col_tiles = nbr_mask.shape[2]
    tile_c = columns // col_tiles
    tokens = tile_f * tile_r * columns
    heads = features // HEAD_DIM
    regs = q_reg.shape[0]
    n_frame, n_row = lax.axis_size("frame"), lax.axis_size("row")
    peers = n_frame * n_row
    share = regs // peers
    with_regs = share % 8 == 0 and 2 * heads <= 128
    nbrs = 0 if n_row == 1 else (1 if n_row == 2 else 2)
    nslot = max(nbrs, 1)
    bias_rows = -(-3 * col_tiles // 8) * 8
    dims = (heads, tokens, columns, tile_c, col_tiles, regs, n_frame, n_row, with_regs)
    bf16, f32 = jnp.bfloat16, jnp.float32
    dma = lambda *shape: pltpu.SemaphoreType.DMA(shape)
    scratch = [
        pltpu.VMEM((regs, features), bf16), pltpu.VMEM((regs, features), bf16),
        pltpu.SMEM(nbr_mask.shape, jnp.int32), dma(4),
        pltpu.VMEM((1 + nbrs, heads, tokens, HEAD_DIM), bf16),
        pltpu.VMEM((3, heads, 2, tokens, HEAD_DIM), bf16),
        pltpu.VMEM((1 + nbrs, bias_rows, tokens), f32),
        pltpu.VMEM((nslot, bias_rows, tokens), f32),
        pltpu.VMEM((3 * tokens, (1 + nbrs) * tokens), f32),
        pltpu.VMEM((heads, HEAD_DIM, tokens), f32),
        pltpu.VMEM((heads, 8, tokens), f32),
        pltpu.VMEM((nslot, heads, HEAD_DIM, tokens), bf16),
        pltpu.VMEM((nslot, heads, 8, tokens), f32),
        pltpu.VMEM((nslot, heads, HEAD_DIM, tokens), bf16),
        pltpu.VMEM((nslot, heads, 8, tokens), f32),
        dma(3, heads), dma(2, heads), dma(2, heads), dma(nslot, heads), dma(nslot, heads),
        dma(nslot), dma(nslot), dma(nslot, heads), dma(nslot, heads), dma(nslot, heads), dma(nslot, heads),
    ]
    out_shape = [jax.ShapeDtypeStruct((tokens, features), bf16)]
    hbm, vmem = (pl.BlockSpec(memory_space=s) for s in (pltpu.HBM, pltpu.VMEM))
    if with_regs:
        scratch += [
            pltpu.VMEM((regs, features), bf16),
            pltpu.VMEM((peers, heads, share, HEAD_DIM), bf16),
            pltpu.VMEM((128, regs), f32),
            pltpu.VMEM((peers, share, 128), f32),
            pltpu.VMEM((peers, heads, share, HEAD_DIM), bf16),
            pltpu.VMEM((peers, share, 128), f32),
            dma(2, peers), dma(2, peers),
        ]
        out_shape.append(jax.ShapeDtypeStruct((share, features), bf16))
        reg_args = (q_reg, k_reg, v_reg)
    else:
        reg_args = (k_reg, v_reg)
    flat = lambda x: x.reshape(tokens, features)
    outs = pl.pallas_call(
        functools.partial(block_kernel, dims),
        out_shape=out_shape,
        in_specs=[hbm] * (4 + len(reg_args)),
        out_specs=[vmem] * len(out_shape),
        scratch_shapes=scratch,
        compiler_params=pltpu.CompilerParams(
            collective_id=0, has_side_effects=True, vmem_limit_bytes=40 * 1024 * 1024),
    )(*(pltpu.with_memory_space_constraint(x, pltpu.HBM) for x in (flat(q_video), flat(k_video), flat(v_video), *reg_args, nbr_mask)))
    out_video = outs[0].reshape(q_video.shape)
    if with_regs:
        out_reg = outs[1]
    else:
        out_reg = registers_by_reduction(q_reg, k_reg, v_reg, k_video, v_video, heads, share)
    return out_video, out_reg


def solution(mesh):
    video = P(("group", "frame"), "row", None, "head")
    reg = P("group", "head")
    return jax.shard_map(
        on_device,
        mesh=mesh,
        in_specs=(video, video, video, reg, reg, reg, P("frame", "row", None, None)),
        out_specs=(video, P(("group", "frame", "row"), "head")),
        check_vma=False,
    )
```

```python
import functools

import jax
import jax.numpy as jnp
from jax import lax
from jax.experimental import pallas as pl
from jax.experimental.pallas import tpu as pltpu
from jax.sharding import PartitionSpec as P

HEAD_DIM = 128
NEG = -1e30
SCALE = HEAD_DIM ** -0.5
LOG2E = 1.4426950408889634
MESH = pl.DeviceIdType.MESH
SLOT_DF = (0, -1, 1)


def offset_index(df, dr, dc):
    code = 9 * (df + 1) + 3 * (dr + 1) + (dc + 1)
    return code - 1 if code > 13 else code


def nt(a, b):
    return lax.dot_general(a, b, (((1,), (1,)), ((), ())), preferred_element_type=jnp.float32)


def tn(a, b):
    return lax.dot_general(a, b, (((0,), (0,)), ((), ())), preferred_element_type=jnp.float32)


def block_kernel(dims, *refs):
    (heads, tokens, columns, tile_c, col_tiles, regs, n_frame, n_row, with_regs) = dims
    peers = n_frame * n_row
    share = regs // peers
    nbrs = 0 if n_row == 1 else (1 if n_row == 2 else 2)
    if with_regs:
        (q_hbm, k_hbm, v_hbm, qr_hbm, kr_hbm, vr_hbm, mask_hbm, out_ref, outr_ref,
         kr_ref, vr_ref, mask_ref, ld_reg, qbuf, kv, bias, bias_out, s_ref, o_own, st_own, o_out, st_out, o_in, st_in,
         ld_sem, zs, zr, xs, xr, bs, br, osd, orv, sts, str_,
         qr_ref, r_out, rst_t, rst_out, r_in, rst_in, rs, rr, relay) = refs
    else:
        (q_hbm, k_hbm, v_hbm, kr_hbm, vr_hbm, mask_hbm, out_ref,
         kr_ref, vr_ref, mask_ref, ld_reg, qbuf, kv, bias, bias_out, s_ref, o_own, st_own, o_out, st_out, o_in, st_in,
         ld_sem, zs, zr, xs, xr, bs, br, osd, orv, sts, str_) = refs
    frame = lax.axis_index("frame")
    row = lax.axis_index("row")
    me = frame * n_row + row
    coef = jnp.float32(SCALE * LOG2E)

    def cols(h):
        return pl.ds(pl.multiple_of(h * HEAD_DIM, HEAD_DIM), HEAD_DIM)

    def load(h):
        return (
            pltpu.make_async_copy(k_hbm.at[:, cols(h)], kv.at[0, h, 0], ld_sem.at[0, h]),
            pltpu.make_async_copy(v_hbm.at[:, cols(h)], kv.at[0, h, 1], ld_sem.at[1, h]),
            pltpu.make_async_copy(q_hbm.at[:, cols(h)], qbuf.at[0, h], ld_sem.at[2, h]),
        )

    for h in range(heads):
        for copy in load(h):
            copy.start()
        if h == 0:
            small = [(mask_hbm, mask_ref), (kr_hbm, kr_ref), (vr_hbm, vr_ref)]
            if with_regs:
                small.append((qr_hbm, qr_ref))
            small = [pltpu.make_async_copy(a, b, ld_reg.at[i]) for i, (a, b) in enumerate(small)]
            for copy in small:
                copy.start()

    frame_links = (
        (1, {"frame": frame + 1}, frame < n_frame - 1, 0),
        (2, {"frame": frame - 1}, frame > 0, 1),
    )
    if nbrs == 0:
        row_links = ()
    elif nbrs == 1:
        row_links = ((0, {"row": 1 - row}, None),)
    else:
        row_links = ((1, {"row": row - 1}, row > 0), (0, {"row": row + 1}, row < n_row - 1))

    def guarded(cond, fn):
        if cond is None:
            fn()
        else:
            pl.when(cond)(fn)

    barrier = pltpu.get_barrier_semaphore()
    links = [(dev, ok, slot - 1) for slot, dev, ok, _ in frame_links]
    links += [(dev, ok, 2 + theirs) for theirs, dev, ok in row_links]
    inbound = [(frame > 0, 0), (frame < n_frame - 1, 1)] + [(row_links[j][2], 2 + j) for j in range(nbrs)]
    for dev, ok, _ in links:
        guarded(ok, lambda dev=dev: pl.semaphore_signal(
            barrier, inc=1, device_id=dev, device_id_type=MESH))
    expected = jnp.int32(0)
    for _, ok, _ in links:
        expected = expected + (1 if ok is None else ok.astype(jnp.int32))
    pl.semaphore_wait(barrier, expected)

    def relay_signal(r):
        for dev, ok, i in links:
            guarded(ok, lambda dev=dev, i=i: pl.semaphore_signal(
                relay.at[r, i], inc=1, device_id=dev, device_id_type=MESH))

    def relay_wait(r):
        for ok, i in inbound:
            guarded(ok, lambda i=i: pl.semaphore_wait(relay.at[r, i], 1))

    def kv_copy(h, link):
        slot, dev, _, i = link
        return pltpu.make_async_remote_copy(
            src_ref=kv.at[0, h], dst_ref=kv.at[slot, h], send_sem=zs.at[i, h],
            recv_sem=zr.at[slot - 1, h], device_id=dev, device_id_type=MESH)

    def q_copy(h, j):
        theirs, dev, _ = row_links[j]
        return pltpu.make_async_remote_copy(
            src_ref=qbuf.at[0, h], dst_ref=qbuf.at[1 + theirs, h], send_sem=xs.at[j, h],
            recv_sem=xr.at[theirs, h], device_id=dev, device_id_type=MESH)

    def bias_copy(j):
        theirs, dev, _ = row_links[j]
        return pltpu.make_async_remote_copy(
            src_ref=bias_out.at[j], dst_ref=bias.at[1 + theirs], send_sem=bs.at[j],
            recv_sem=br.at[theirs], device_id=dev, device_id_type=MESH)

    def o_copy(h, j):
        theirs, dev, _ = row_links[j]
        return (
            pltpu.make_async_remote_copy(
                src_ref=o_out.at[j, h], dst_ref=o_in.at[theirs, h], send_sem=osd.at[j, h],
                recv_sem=orv.at[theirs, h], device_id=dev, device_id_type=MESH),
            pltpu.make_async_remote_copy(
                src_ref=st_out.at[j, h], dst_ref=st_in.at[theirs, h], send_sem=sts.at[j, h],
                recv_sem=str_.at[theirs, h], device_id=dev, device_id_type=MESH),
        )

    for h in range(heads):
        copies = load(h)
        copies[0].wait()
        copies[1].wait()
        for link in frame_links:
            guarded(link[2], lambda link=link: kv_copy(h, link).start())
        copies[2].wait()
        for j in range(nbrs):
            guarded(row_links[j][2], lambda j=j: q_copy(h, j).start())

    for copy in small:
        copy.wait()

    lane_tile = (lax.broadcasted_iota(jnp.int32, (1, tokens), 1) % columns) // tile_c
    frame_ok = [None, (frame > 0).astype(jnp.int32), (frame < n_frame - 1).astype(jnp.int32)]
    bias[0] = jnp.zeros(bias.shape[1:], bias.dtype)
    if nbrs:
        bias_out[...] = jnp.zeros_like(bias_out)
    for target in range(1 + nbrs):
        for slot, df in enumerate(SLOT_DF):
            for tk in range(col_tiles):
                vec = jnp.full((1, tokens), NEG, jnp.float32)
                for tq in range(col_tiles):
                    dc = tk - tq
                    if abs(dc) > 1:
                        continue
                    if target == 0:
                        if df == 0 and dc == 0:
                            ok = jnp.int32(1)
                        else:
                            ok = mask_ref[0, 0, tq, offset_index(df, 0, dc)]
                    elif nbrs == 1:
                        plus, minus = offset_index(df, 1, dc), offset_index(df, -1, dc)
                        ok = mask_ref[0, 0, tq, plus + row * (minus - plus)]
                    else:
                        ok = mask_ref[0, 0, tq, offset_index(df, (-1, 1)[target - 1], dc)]
                    if frame_ok[slot] is not None:
                        ok = ok * frame_ok[slot]
                    vec = jnp.where(lane_tile == tq, (ok.astype(jnp.float32) - 1.0) * -NEG, vec)
                r = slot * col_tiles + tk
                if target == 0:
                    bias[0, r:r + 1, :] = vec
                else:
                    bias_out[target - 1, r:r + 1, :] = vec
    for j in range(nbrs):
        guarded(row_links[j][2], lambda j=j: bias_copy(j).start())

    @pl.when(frame == 0)
    def _():
        kv[1] = jnp.zeros(kv.shape[1:], kv.dtype)

    @pl.when(frame == n_frame - 1)
    def _():
        kv[2] = jnp.zeros(kv.shape[1:], kv.dtype)

    for j in range(nbrs):
        if row_links[j][2] is not None:
            @pl.when(jnp.logical_not(row_links[j][2]))
            def _():
                qbuf[1 + j] = jnp.zeros(qbuf.shape[1:], qbuf.dtype)
                bias[1 + j] = jnp.zeros(bias.shape[1:], bias.dtype)

    if with_regs:
        own_lane = lax.broadcasted_iota(jnp.int32, (1, regs), 1) // share == me
        reg_bias = jnp.where(own_lane, 0.0, NEG).astype(jnp.float32)

        def reg_head(h, carry):
            qh = qr_ref[:, cols(h)]
            s0 = nt(kv[0, h, 0], qh) * coef
            s1 = nt(kr_ref[:, cols(h)], qh) * coef + reg_bias
            m = jnp.maximum(jnp.max(s0, 0, keepdims=True), jnp.max(s1, 0, keepdims=True))
            p0 = jnp.exp2(s0 - m)
            p1 = jnp.exp2(s1 - m)
            l = jnp.sum(p0, 0, keepdims=True) + jnp.sum(p1, 0, keepdims=True)
            acc = tn(kv[0, h, 1], p0.astype(jnp.bfloat16)) + tn(vr_ref[:, cols(h)], p1.astype(jnp.bfloat16))
            r_out[:, h] = acc.T.reshape(peers, share, HEAD_DIM).astype(jnp.bfloat16)
            rst_t[pl.ds(h, 1), :] = m
            rst_t[pl.ds(heads + h, 1), :] = l
            return carry

        rst_t[...] = jnp.zeros_like(rst_t)
        rounds = max(n_frame + n_row - 3, 0)
        done = 0
        for r in range(rounds):
            relay_signal(r)
            upto = heads * (r + 1) // rounds
            lax.fori_loop(done, upto, reg_head, 0)
            done = upto
            relay_wait(r)
        lax.fori_loop(done, heads, reg_head, 0)
        rst_out[...] = rst_t[...].T.reshape(rst_out.shape)

        def reg_copy(k):
            peer = lax.rem(me + k, peers)
            dev = {"frame": peer // n_row, "row": lax.rem(peer, n_row)}
            return (
                pltpu.make_async_remote_copy(
                    src_ref=r_out.at[peer], dst_ref=r_in.at[k], send_sem=rs.at[0, k],
                    recv_sem=rr.at[0, k], device_id=dev, device_id_type=MESH),
                pltpu.make_async_remote_copy(
                    src_ref=rst_out.at[peer], dst_ref=rst_in.at[k], send_sem=rs.at[1, k],
                    recv_sem=rr.at[1, k], device_id=dev, device_id_type=MESH),
            )

        for k in range(1, peers):
            for copy in reg_copy(k):
                copy.start()

    for j in range(nbrs):
        guarded(row_links[j][2], lambda j=j: pltpu.make_async_remote_copy(
            src_ref=bias_out.at[j], dst_ref=bias.at[1 + j], send_sem=bs.at[j], recv_sem=br.at[j],
            device_id=row_links[j][1], device_id_type=MESH).wait_recv())

    lanes = (1 + nbrs) * tokens

    def video_head(h, carry):
        for j in range(nbrs):
            guarded(row_links[j][2], lambda j=j: pltpu.make_async_remote_copy(
                src_ref=qbuf.at[0, h], dst_ref=qbuf.at[1 + j, h], send_sem=xs.at[j, h],
                recv_sem=xr.at[j, h], device_id=row_links[j][1], device_id_type=MESH).wait_recv())
        qall = qbuf[:, h].reshape(lanes, HEAD_DIM)
        m = None
        for slot in range(3):
            if slot:
                there = (frame > 0) if slot == 1 else (frame < n_frame - 1)
                dev = {"frame": frame - 1} if slot == 1 else {"frame": frame + 1}
                guarded(there, lambda: pltpu.make_async_remote_copy(
                    src_ref=kv.at[0, h], dst_ref=kv.at[slot, h], send_sem=zs.at[slot - 1, h],
                    recv_sem=zr.at[slot - 1, h], device_id=dev, device_id_type=MESH).wait_recv())
            s = nt(kv[slot, h, 0], qall) * coef
            rows = bias[:, slot * col_tiles:(slot + 1) * col_tiles, :]
            rows = jnp.concatenate([rows[t] for t in range(1 + nbrs)], axis=1)
            s = s.reshape(tokens // columns, col_tiles, tile_c, lanes) + rows[None, :, None, :]
            s = s.reshape(tokens, lanes)
            s_ref[slot * tokens:(slot + 1) * tokens, :] = s
            top = jnp.max(s, 0, keepdims=True)
            m = top if m is None else jnp.maximum(m, top)
        sr = nt(kr_ref[:, cols(h)], qall[:tokens]) * coef
        m_own = jnp.maximum(m[:, :tokens], jnp.max(sr, 0, keepdims=True))
        m = jnp.concatenate([m_own, m[:, tokens:]], axis=1) if nbrs else m_own
        pr = jnp.exp2(sr - m_own)
        l = None
        o = None
        for slot in range(3):
            p = jnp.exp2(s_ref[slot * tokens:(slot + 1) * tokens, :] - m)
            total = jnp.sum(p, 0, keepdims=True)
            part = tn(kv[slot, h, 1], p.astype(jnp.bfloat16))
            l = total if l is None else l + total
            o = part if o is None else o + part
        for j in range(nbrs):
            sl = slice((1 + j) * tokens, (2 + j) * tokens)
            o_out[j, h] = o[:, sl].astype(jnp.bfloat16)
            st_out[j, h] = jnp.concatenate([m[:, sl]] * 4 + [l[:, sl]] * 4, axis=0)

            def send(j=j):
                for copy in o_copy(h, j):
                    copy.start()

            guarded(row_links[j][2], send)
        o_own[h] = o[:, :tokens] + tn(vr_ref[:, cols(h)], pr.astype(jnp.bfloat16))
        l_own = l[:, :tokens] + jnp.sum(pr, 0, keepdims=True)
        st_own[h] = jnp.concatenate([m_own] * 4 + [l_own] * 4, axis=0)
        return carry

    for j in range(nbrs):
        if row_links[j][2] is not None:
            @pl.when(jnp.logical_not(row_links[j][2]))
            def _():
                o_in[j] = jnp.zeros(o_in.shape[1:], o_in.dtype)
                st_in[j] = jnp.full(st_in.shape[1:], NEG, st_in.dtype)

    lax.fori_loop(0, heads, video_head, 0)

    def finish_head(h, carry):
        st = st_own[h]
        m, l, o = st[0:1], st[4:5], o_own[h]
        parts = []
        for j in range(nbrs):
            def arrive(j=j):
                pltpu.make_async_remote_copy(
                    src_ref=o_out.at[j, h], dst_ref=o_in.at[j, h], send_sem=osd.at[j, h],
                    recv_sem=orv.at[j, h], device_id=row_links[j][1], device_id_type=MESH).wait_recv()
                pltpu.make_async_remote_copy(
                    src_ref=st_out.at[j, h], dst_ref=st_in.at[j, h], send_sem=sts.at[j, h],
                    recv_sem=str_.at[j, h], device_id=row_links[j][1], device_id_type=MESH).wait_recv()

            guarded(row_links[j][2], arrive)
            other = st_in[j, h]
            parts.append((other[0:1], other[4:5], o_in[j, h].astype(jnp.float32)))
        joint = m
        for mj, _, _ in parts:
            joint = jnp.maximum(joint, mj)
        factor = jnp.exp2(m - joint)
        total = l * factor
        factors = []
        for mj, lj, _ in parts:
            fj = jnp.exp2(mj - joint)
            factors.append(fj)
            total = total + lj * fj
        inv = 1.0 / total
        o = o * (factor * inv)
        for fj, (_, _, oj) in zip(factors, parts):
            o = o + oj * (fj * inv)
        out_ref[:, cols(h)] = o.T.astype(jnp.bfloat16)
        return carry

    lax.fori_loop(0, heads - 1, finish_head, 0)

    if with_regs:
        for k in range(1, peers):
            for copy in reg_copy(k):
                copy.wait_recv()
        for h in range(heads):
            ms = [rst_out[me][:, h:h + 1]] + [rst_in[k][:, h:h + 1] for k in range(1, peers)]
            ls = [rst_out[me][:, heads + h:heads + h + 1]] + [
                rst_in[k][:, heads + h:heads + h + 1] for k in range(1, peers)]
            accs = [r_out[me, h]] + [r_in[k, h] for k in range(1, peers)]
            joint = functools.reduce(jnp.maximum, ms)
            total = None
            acc = None
            for mk, lk, ak in zip(ms, ls, accs):
                f = jnp.exp2(mk - joint)
                tk, wk = lk * f, ak.astype(jnp.float32) * f
                total = tk if total is None else total + tk
                acc = wk if acc is None else acc + wk
            outr_ref[:, h * HEAD_DIM:(h + 1) * HEAD_DIM] = (acc / total).astype(jnp.bfloat16)

    lax.fori_loop(heads - 1, heads, finish_head, 0)

    def sent(h, carry):
        for link in frame_links:
            guarded(link[2], lambda link=link: kv_copy(h, link).wait_send())
        for j in range(nbrs):
            def left(j=j):
                q_copy(h, j).wait_send()
                for copy in o_copy(h, j):
                    copy.wait_send()

            guarded(row_links[j][2], left)
        return carry

    lax.fori_loop(0, heads, sent, 0)
    for j in range(nbrs):
        guarded(row_links[j][2], lambda j=j: bias_copy(j).wait_send())
    if with_regs:
        for k in range(1, peers):
            for copy in reg_copy(k):
                copy.wait_send()


def exact_product(weights, values):
    leading = weights.astype(values.dtype)
    remainder = (weights - leading.astype(weights.dtype)).astype(values.dtype)
    return jnp.einsum("hqk,khd->hqd", leading, values, preferred_element_type=jnp.float32) + jnp.einsum(
        "hqk,khd->hqd", remainder, values, preferred_element_type=jnp.float32)


def partial_softmax(queries, keys, values):
    scores = jnp.einsum("qhd,khd->hqk", queries, keys, preferred_element_type=jnp.float32) * SCALE
    top = jnp.max(scores, axis=-1)
    weights = jnp.exp(scores - top[..., None])
    return top, jnp.sum(weights, axis=-1), exact_product(weights, values)


def registers_by_reduction(q_reg, k_reg, v_reg, k_video, v_video, heads, share):
    split = lambda x: x.reshape(-1, heads, HEAD_DIM)
    start = (lax.axis_index("frame") * lax.axis_size("row") + lax.axis_index("row")) * share
    top, total, weighted = partial_softmax(split(q_reg), split(k_video), split(v_video))
    joint = lax.pmax(top, ("frame", "row"))
    factor = jnp.exp(top - joint)
    total, weighted = lax.psum((total * factor, weighted * factor[..., None]), ("frame", "row"))
    own = lambda x: lax.dynamic_slice_in_dim(x, start, share, 1)
    queries = lax.dynamic_slice_in_dim(q_reg, start, share, 0)
    top2, total2, weighted2 = partial_softmax(split(queries), split(k_reg), split(v_reg))
    top1, total1, weighted1 = own(joint), own(total), own(weighted)
    last = jnp.maximum(top1, top2)
    f1, f2 = jnp.exp(top1 - last), jnp.exp(top2 - last)
    out = (weighted1 * f1[..., None] + weighted2 * f2[..., None]) / (total1 * f1 + total2 * f2)[..., None]
    return out.transpose(1, 0, 2).reshape(share, heads * HEAD_DIM).astype(jnp.bfloat16)


def on_device(q_video, k_video, v_video, q_reg, k_reg, v_reg, nbr_mask):
    tile_f, tile_r, columns, features = q_video.shape
    col_tiles = nbr_mask.shape[2]
    tile_c = columns // col_tiles
    tokens = tile_f * tile_r * columns
    heads = features // HEAD_DIM
    regs = q_reg.shape[0]
    n_frame, n_row = lax.axis_size("frame"), lax.axis_size("row")
    peers = n_frame * n_row
    share = regs // peers
    with_regs = share % 8 == 0 and 2 * heads <= 128
    nbrs = 0 if n_row == 1 else (1 if n_row == 2 else 2)
    nslot = max(nbrs, 1)
    bias_rows = -(-3 * col_tiles // 8) * 8
    dims = (heads, tokens, columns, tile_c, col_tiles, regs, n_frame, n_row, with_regs)
    bf16, f32 = jnp.bfloat16, jnp.float32
    dma = lambda *shape: pltpu.SemaphoreType.DMA(shape)
    scratch = [
        pltpu.VMEM((regs, features), bf16), pltpu.VMEM((regs, features), bf16),
        pltpu.SMEM(nbr_mask.shape, jnp.int32), dma(4),
        pltpu.VMEM((1 + nbrs, heads, tokens, HEAD_DIM), bf16),
        pltpu.VMEM((3, heads, 2, tokens, HEAD_DIM), bf16),
        pltpu.VMEM((1 + nbrs, bias_rows, tokens), f32),
        pltpu.VMEM((nslot, bias_rows, tokens), f32),
        pltpu.VMEM((3 * tokens, (1 + nbrs) * tokens), f32),
        pltpu.VMEM((heads, HEAD_DIM, tokens), f32),
        pltpu.VMEM((heads, 8, tokens), f32),
        pltpu.VMEM((nslot, heads, HEAD_DIM, tokens), bf16),
        pltpu.VMEM((nslot, heads, 8, tokens), f32),
        pltpu.VMEM((nslot, heads, HEAD_DIM, tokens), bf16),
        pltpu.VMEM((nslot, heads, 8, tokens), f32),
        dma(3, heads), dma(2, heads), dma(2, heads), dma(nslot, heads), dma(nslot, heads),
        dma(nslot), dma(nslot), dma(nslot, heads), dma(nslot, heads), dma(nslot, heads), dma(nslot, heads),
    ]
    out_shape = [jax.ShapeDtypeStruct((tokens, features), bf16)]
    hbm, vmem = (pl.BlockSpec(memory_space=s) for s in (pltpu.HBM, pltpu.VMEM))
    if with_regs:
        scratch += [
            pltpu.VMEM((regs, features), bf16),
            pltpu.VMEM((peers, heads, share, HEAD_DIM), bf16),
            pltpu.VMEM((128, regs), f32),
            pltpu.VMEM((peers, share, 128), f32),
            pltpu.VMEM((peers, heads, share, HEAD_DIM), bf16),
            pltpu.VMEM((peers, share, 128), f32),
            dma(2, peers), dma(2, peers),
            pltpu.SemaphoreType.REGULAR((max(n_frame + n_row - 3, 1), 4)),
        ]
        out_shape.append(jax.ShapeDtypeStruct((share, features), bf16))
        reg_args = (q_reg, k_reg, v_reg)
    else:
        reg_args = (k_reg, v_reg)
    flat = lambda x: x.reshape(tokens, features)
    outs = pl.pallas_call(
        functools.partial(block_kernel, dims),
        out_shape=out_shape,
        in_specs=[hbm] * (4 + len(reg_args)),
        out_specs=[vmem] * len(out_shape),
        scratch_shapes=scratch,
        compiler_params=pltpu.CompilerParams(
            collective_id=0, has_side_effects=True, vmem_limit_bytes=40 * 1024 * 1024),
    )(*(pltpu.with_memory_space_constraint(x, pltpu.HBM) for x in (flat(q_video), flat(k_video), flat(v_video), *reg_args, nbr_mask)))
    out_video = outs[0].reshape(q_video.shape)
    if with_regs:
        out_reg = outs[1]
    else:
        out_reg = registers_by_reduction(q_reg, k_reg, v_reg, k_video, v_video, heads, share)
    return out_video, out_reg


def solution(mesh):
    video = P(("group", "frame"), "row", None, "head")
    reg = P("group", "head")
    return jax.shard_map(
        on_device,
        mesh=mesh,
        in_specs=(video, video, video, reg, reg, reg, P("frame", "row", None, None)),
        out_specs=(video, P(("group", "frame", "row"), "head")),
        check_vma=False,
    )
```
